256 devices in a mesh: grp: 8 (over x, core), uly: 32 (over z, y).
Axes of the slice: x: 4, y: 4, z: 8, core: 2. Of those that a mesh axis runs over, the one named last changes fastest.
Arguments:
- queries: bfloat16 [32768, 8192], P(('grp', 'uly')), may hold values from -6 to 6
- key_state_rows: bfloat16 [32768, 1024], P(('grp', 'uly')), may hold values from -6 to 6
- value_state_rows: bfloat16 [32768, 1024], P(('grp', 'uly')), may hold values from -6 to 6
- vert_blocks: int32 [64, 6], replicated, may hold values from -1 to 255, as said below
- slash_offsets: int32 [64, 3], replicated, may hold values from -1 to 16, as said below
Outputs:
- attended: bfloat16 [32768, 8192], P(('grp', 'uly'))
The draws below stay inside these ranges and needn't reach their ends.
Inputs may be any that keep to these rules, and one draw needn't show every extreme that they name: `vert_blocks`: row h lists distinct block numbers first and -1 in the slots after them; every row lists one block or more and some row lists 6. `slash_offsets`: row h lists distinct offsets of at least 1 first and -1 in the slots after them; every row lists one offset or more and some row lists 3.
All inputs are finite; a program needn't handle non-finite values.
Results may differ from the reference program's by a relative error of at most 0.005.
Values may be sent and summed in bfloat16 or wider, within the bound.
No kernel may reach another device: no remote copies, remote signals or barrier semaphores. Data moves between devices by JAX's collectives and lax.ppermute only.
A program may use at most 128 MiB of HBM per device.

```python
import jax
import jax.numpy as jnp
from jax import lax

QUERY_HEADS = 64
KEY_VALUE_HEADS = 8
HEAD_SIZE = 128
BLOCK_TOKENS = 128
NV = 6
NS = 3
TOTAL_TOKENS = 32768
NBLK = 256
SPAN = 16


def draw_queries(key, part):
    random_jitter = jax.random.normal(jax.random.fold_in(key, 1), (TOTAL_TOKENS, QUERY_HEADS, HEAD_SIZE), dtype=jnp.float32)
    random_jitter = jnp.clip(random_jitter, -6.0, 6.0)
    return random_jitter.reshape(TOTAL_TOKENS, QUERY_HEADS * HEAD_SIZE).astype(jnp.bfloat16)


def draw_key_state_rows(key, part):
    random_jitter = jax.random.normal(jax.random.fold_in(key, 2), (TOTAL_TOKENS, KEY_VALUE_HEADS, HEAD_SIZE), dtype=jnp.float32)
    random_jitter = jnp.clip(random_jitter, -6.0, 6.0)
    return random_jitter.reshape(TOTAL_TOKENS, KEY_VALUE_HEADS * HEAD_SIZE).astype(jnp.bfloat16)


def draw_vert_blocks(key, part):
    head_keys = jax.random.split(jax.random.fold_in(key, 11), QUERY_HEADS)

    def pick_blocks(head_key):
        return jax.random.permutation(head_key, NBLK)[:NV]
    picks = jax.vmap(pick_blocks)(head_keys).astype(jnp.int32)
    heavy = jax.random.randint(jax.random.fold_in(key, 12), (QUERY_HEADS,), 0, 4) == 0
    lighter = jax.random.randint(jax.random.fold_in(key, 13), (QUERY_HEADS,), 1, 3)
    full_head = jax.random.randint(jax.random.fold_in(key, 14), (), 0, QUERY_HEADS)
    counts = jnp.where(heavy | (jnp.arange(QUERY_HEADS) == full_head), NV, lighter)
    return jnp.where(jnp.arange(NV)[None, :] < counts[:, None], picks, -1).astype(jnp.int32)


def draw_slash_offsets(key, part):
    head_keys = jax.random.split(jax.random.fold_in(key, 21), QUERY_HEADS)

    def pick_offsets(head_key):
        return jax.random.permutation(head_key, SPAN)[:NS] + 1
    picks = jax.vmap(pick_offsets)(head_keys).astype(jnp.int32)
    counts = jax.random.randint(jax.random.fold_in(key, 22), (QUERY_HEADS,), 1, NS + 1)
    full_head = jax.random.randint(jax.random.fold_in(key, 23), (), 0, QUERY_HEADS)
    counts = jnp.where(jnp.arange(QUERY_HEADS) == full_head, NS, counts)
    return jnp.where(jnp.arange(NS)[None, :] < counts[:, None], picks, -1).astype(jnp.int32)


def steps_of(stream_key, extent, cuts, low, top_value):
    level = 1.0
    for position, blocks in cuts:
        draws = jax.random.uniform(jax.random.fold_in(jax.random.fold_in(stream_key, 6), position), (blocks,), jnp.float32, low / len(cuts), top_value / len(cuts))
        level = level * jnp.repeat(jnp.exp(draws), extent[position] // blocks).reshape((-1,) + (1,) * (len(extent) - 1 - position))
    return level


def gaussian(key, shape, width, limit, cuts=(), kind=jnp.bfloat16):
    values = width * jax.random.normal(key, shape, jnp.float32)
    if cuts:
        values = values * steps_of(key, shape, cuts, -0.22, 0.18)
    return jnp.clip(values, -limit, limit).astype(kind)


def setup_inputs(seed: int = 0) -> dict:
    streams_of = jax.random.split(jax.random.key(seed), 6)
    return {
        "queries": draw_queries(jax.random.fold_in(streams_of[5], 71), 0),
        "key_state_rows": draw_key_state_rows(jax.random.fold_in(streams_of[5], 71), 0),
        "value_state_rows": gaussian(streams_of[2], (TOTAL_TOKENS, KEY_VALUE_HEADS * HEAD_SIZE), 1.0, 6.0, ((0, 256),)),
        "vert_blocks": draw_vert_blocks(jax.random.fold_in(streams_of[5], 71), 0),
        "slash_offsets": draw_slash_offsets(jax.random.fold_in(streams_of[5], 71), 0),
    }


neg_large = -1.0e30


def reference(queries, key_state_rows, value_state_rows, vert_blocks, slash_offsets):
    group_width = QUERY_HEADS // KEY_VALUE_HEADS
    total_blocks = TOTAL_TOKENS // BLOCK_TOKENS
    score_scale = HEAD_SIZE ** -0.5
    q_tiles = queries.reshape(total_blocks, BLOCK_TOKENS, QUERY_HEADS, HEAD_SIZE)
    key_block_tiles = key_state_rows.reshape(total_blocks, BLOCK_TOKENS, KEY_VALUE_HEADS, HEAD_SIZE)
    value_block_tiles = value_state_rows.reshape(total_blocks, BLOCK_TOKENS, KEY_VALUE_HEADS, HEAD_SIZE)
    blocks = jnp.arange(total_blocks, dtype=jnp.int32)
    causal = jnp.arange(BLOCK_TOKENS)[:, None] >= jnp.arange(BLOCK_TOKENS)[None, :]
    slot_total = 1 + NS + NV
    first_slot = jnp.arange(slot_total) == 0

    def one_head(head_index):
        kv_head = head_index // group_width
        q_head = lax.dynamic_index_in_dim(q_tiles, head_index, axis=2, keepdims=False).astype(jnp.float32)
        k_head = lax.dynamic_index_in_dim(key_block_tiles, kv_head, axis=2, keepdims=False)
        v_head = lax.dynamic_index_in_dim(value_block_tiles, kv_head, axis=2, keepdims=False)
        offset_list = lax.dynamic_index_in_dim(slash_offsets, head_index, axis=0, keepdims=False)
        vert_list = lax.dynamic_index_in_dim(vert_blocks, head_index, axis=0, keepdims=False)
        targets = blocks[:, None] - offset_list[None, :]
        slash_ok = (offset_list[None, :] >= 1) & (targets >= 0)
        hits = slash_ok[:, :, None] & (targets[:, :, None] == vert_list[None, None, :])
        vert_ok = (vert_list[None, :] >= 0) & (vert_list[None, :] < blocks[:, None]) & jnp.logical_not(jnp.any(hits, axis=1))
        vert_full = jnp.broadcast_to(vert_list[None, :], (total_blocks, NV))
        chosen = jnp.concatenate([blocks[:, None], jnp.where(slash_ok, targets, 0), jnp.where(vert_ok, vert_full, 0)], axis=1).astype(jnp.int32)
        allowed = jnp.concatenate([jnp.ones((total_blocks, 1), dtype=bool), slash_ok, vert_ok], axis=1)
        k_sel = k_head[chosen].astype(jnp.float32)
        v_sel = v_head[chosen].astype(jnp.float32)
        scores = jnp.einsum("nqd,nskd->nqsk", q_head, k_sel) * score_scale
        keep_mask = allowed[:, None, :, None] & (causal[None, :, None, :] | jnp.logical_not(first_slot)[None, None, :, None])
        scores = jnp.where(keep_mask, scores, neg_large)
        row_best = jnp.max(scores, axis=(2, 3), keepdims=True)
        weights = jnp.where(keep_mask, jnp.exp(scores - row_best), 0.0)
        total = jnp.sum(weights, axis=(2, 3))
        probs_low = weights.astype(jnp.bfloat16).astype(jnp.float32)
        summed = jnp.einsum("nqsk,nskd->nqd", probs_low, v_sel)
        return (summed / total[:, :, None]).astype(jnp.bfloat16)

    heads_out = lax.map(one_head, jnp.arange(QUERY_HEADS, dtype=jnp.int32))
    return heads_out.transpose(1, 2, 0, 3).reshape(TOTAL_TOKENS, QUERY_HEADS * HEAD_SIZE)
```

```python
import functools

import jax
import jax.numpy as jnp
import numpy as np
from jax import lax
from jax.experimental import pallas as pl
from jax.experimental.pallas import tpu as pltpu
from jax.sharding import Mesh, PartitionSpec as P

QUERY_HEADS = 64
KEY_VALUE_HEADS = 8
HEAD_SIZE = 128
BLOCK_TOKENS = 128
NV = 6
NS = 3
SPAN = 16

CHIPS_X, CORES, CHIPS_Z, CHIPS_Y = 4, 2, 8, 4
ALL_AXES = ("x", "c", "z", "y")
HEAD_AXES = ("c", "y")
ROW_AXES = ("x", "z")
PARTS = CORES * CHIPS_Y
GROUP = QUERY_HEADS // KEY_VALUE_HEADS
ROW = CHIPS_Y
STEPS = SPAN // ROW
WINDOW = SPAN + ROW
SLICES = CHIPS_X * CHIPS_Z
PAIR_ROWS = 2 * BLOCK_TOKENS
SLICE_ROWS = PAIR_ROWS // SLICES
PICKS = GROUP * NV
SLOTS = 1 + NS + NV
TILES = CORES * WINDOW + PICKS

NEG = -1e30
LOG2_SCALE = float(HEAD_SIZE**-0.5 * np.log2(np.e))


def attend_kernel(turns, tile_of, bias_of, q_ref, *rest):
    near = rest[: 1 + 2 * STEPS]
    vert_ref, out_ref, tiles, sem = rest[1 + 2 * STEPS :]
    head = pl.program_id(0)

    @pl.when(head == 0)
    def _():
        copies = []
        for run in range(CORES):
            first = run * WINDOW
            copies.append((near[0].at[run], tiles.at[pl.ds(first + SPAN, ROW)]))
            for step in range(STEPS):
                source = near[1 + 2 * step + run]
                at = first + SPAN - ROW * (step + 1)
                copies.append((source, tiles.at[pl.ds(at, ROW)]))
        for part in range(SLICES):
            target = tiles.at[
                pl.ds(CORES * WINDOW, PICKS), pl.ds(part * SLICE_ROWS, SLICE_ROWS)
            ]
            copies.append((vert_ref.at[part], target))
        copies = [
            pltpu.make_async_copy(source, target, sem.at[n])
            for n, (source, target) in enumerate(copies)
        ]
        for copy in copies:
            copy.start()
        for copy in copies:
            copy.wait()

    rows = lax.broadcasted_iota(jnp.int32, (BLOCK_TOKENS, BLOCK_TOKENS), 0)
    cols = lax.broadcasted_iota(jnp.int32, (BLOCK_TOKENS, BLOCK_TOKENS), 1)
    causal = rows >= cols

    def attend(block, count):
        base = (head * PARTS + block) * SLOTS
        where = [tile_of[base + slot] for slot in range(count)]
        keys = jnp.concatenate([tiles[w, :BLOCK_TOKENS, :] for w in where], axis=0)
        values = jnp.concatenate([tiles[w, BLOCK_TOKENS:, :] for w in where], axis=0)
        raw = lax.dot_general(
            q_ref[block], keys, (((1,), (1,)), ((), ())), preferred_element_type=jnp.float32
        )
        scores = [raw[:, s * BLOCK_TOKENS : (s + 1) * BLOCK_TOKENS] for s in range(count)]
        scores[0] = jnp.where(causal, scores[0], NEG)
        for slot in range(1, count):
            scores[slot] = scores[slot] + bias_of[base + slot]
        best = jnp.max(functools.reduce(jnp.maximum, scores), axis=1, keepdims=True)
        weights = [jnp.exp2((s - best) * LOG2_SCALE) for s in scores]
        total = jnp.sum(functools.reduce(jnp.add, weights), axis=1, keepdims=True)
        probs = jnp.concatenate([w.astype(jnp.bfloat16) for w in weights], axis=1)
        mixed = jnp.dot(probs, values, preferred_element_type=jnp.float32)
        out_ref[block] = (mixed * (1.0 / total)).astype(jnp.bfloat16)

    for count in range(2, SLOTS + 1, 2):

        @pl.when(turns[head] == count)
        def _():
            @pl.loop(0, CORES)
            def _(run):
                for place in range(ROW):
                    attend(run * ROW + place, count)


def attend_all(turns, tile_of, bias_of, q, near, vert):
    head_spec = pl.BlockSpec(
        (PARTS, BLOCK_TOKENS, HEAD_SIZE), lambda head, *_: (0, 0, head)
    )
    anywhere = pl.BlockSpec(memory_space=pl.ANY)
    return pl.pallas_call(
        attend_kernel,
        out_shape=jax.ShapeDtypeStruct(q.shape, jnp.bfloat16),
        grid_spec=pltpu.PrefetchScalarGridSpec(
            num_scalar_prefetch=3,
            grid=(GROUP,),
            in_specs=[head_spec] + [anywhere] * (len(near) + 1),
            out_specs=head_spec,
            scratch_shapes=[
                pltpu.VMEM((TILES, PAIR_ROWS, HEAD_SIZE), jnp.bfloat16),
                pltpu.SemaphoreType.DMA((CORES * (1 + STEPS) + SLICES,)),
            ],
        ),
        compiler_params=pltpu.CompilerParams(
            dimension_semantics=("arbitrary",), vmem_limit_bytes=40 << 20
        ),
        cost_estimate=pl.CostEstimate(
            flops=4 * 64 * 6 * 128**3, bytes_accessed=10 << 20, transcendentals=64 * 6 * 128**2
        ),
        name="attend",
    )(turns, tile_of, bias_of, q, *near, vert)


def slot_tables(vert, slash, first_blocks):
    slash_count = jnp.sum((slash >= 1).astype(jnp.int32), axis=1)
    vert_count = jnp.sum((vert >= 0).astype(jnp.int32), axis=1)
    turns = 1 + slash_count + vert_count
    turns = (turns + 1) // 2 * 2
    part = np.arange(PARTS)
    numbers = first_blocks[part // ROW] + (part % ROW)
    own = jnp.asarray(part // ROW * WINDOW + SPAN + part % ROW, jnp.int32)
    near_tile = own[None, :, None] - jnp.maximum(slash, 0)[:, None, :]
    near_ok = (slash[:, None, :] >= 1) & (numbers[None, :, None] >= slash[:, None, :])
    far_tile = CORES * WINDOW + np.arange(PICKS, dtype=np.int32).reshape(GROUP, 1, NV)
    far_tile = jnp.broadcast_to(far_tile, (GROUP, PARTS, NV))
    hit = jnp.any(
        near_ok[:, :, :, None]
        & (
            numbers[None, :, None, None] - slash[:, None, :, None]
            == vert[:, None, None, :]
        ),
        axis=2,
    )
    far_ok = (
        (vert[:, None, :] >= 0)
        & (vert[:, None, :] < numbers[None, :, None])
        & jnp.logical_not(hit)
    )
    own_tile = jnp.broadcast_to(own[None, :, None], (GROUP, PARTS, 1))
    tile = jnp.concatenate([own_tile, near_tile, far_tile], axis=2)
    fine = jnp.concatenate([jnp.ones((GROUP, PARTS, 1), bool), near_ok, far_ok], axis=2)
    slot = np.arange(SLOTS)
    listed = jnp.concatenate(
        [jnp.ones((GROUP, 1), bool), slash >= 1, vert >= 0], axis=1
    )
    place = jnp.cumsum(listed.astype(jnp.int32), axis=1) - 1
    chosen = listed[:, :, None] & (place[:, :, None] == slot[None, None, :])
    chosen = chosen[:, None, :, :]
    tile_of = jnp.sum(jnp.where(chosen, tile[:, :, :, None], 0), axis=2)
    good = jnp.any(chosen & fine[:, :, :, None], axis=2)
    bias_of = jnp.where(good, 0.0, NEG).astype(jnp.float32)
    return turns, tile_of.reshape(-1), bias_of.reshape(-1)


def shards(queries, key_state_rows, value_state_rows, vert_blocks, slash_offsets):
    x, z = lax.axis_index("x"), lax.axis_index("z")
    key_head = lax.axis_index("c") * CHIPS_Y + lax.axis_index("y")
    tokens = BLOCK_TOKENS

    def by_head(rows, width):
        return rows.reshape(tokens, KEY_VALUE_HEADS, width).transpose(1, 0, 2)

    pairs = jnp.concatenate(
        [by_head(key_state_rows, HEAD_SIZE), by_head(value_state_rows, HEAD_SIZE)], axis=1
    )
    pairs = lax.all_to_all(pairs, HEAD_AXES, 0, 0, tiled=True)
    own = pairs.reshape(CORES, ROW, PAIR_ROWS, HEAD_SIZE)

    last = z == CHIPS_Z - 1
    on = [(n, n + 1) for n in range(SLICES - 1)]
    around = [
        (a * CHIPS_Z + b, a * CHIPS_Z + (b + 1) % CHIPS_Z)
        for a in range(CHIPS_X)
        for b in range(CHIPS_Z)
    ]
    near = [own]
    even, odd = own[0], own[1]
    for _ in range(STEPS):
        to_even = jnp.where(last, odd, even)
        to_odd = jnp.where(last, even, odd)
        even = lax.ppermute(to_even, ROW_AXES, on)
        odd = lax.ppermute(to_odd, ROW_AXES, around)
        near += [even, odd]

    sliced = pairs.reshape(PARTS, SLICES, SLICE_ROWS, HEAD_SIZE).transpose(1, 0, 2, 3)
    sliced = lax.all_to_all(sliced, ROW_AXES, 0, 0, tiled=True)
    vert = lax.dynamic_slice_in_dim(vert_blocks, key_head * GROUP, GROUP, 0)
    slash = lax.dynamic_slice_in_dim(slash_offsets, key_head * GROUP, GROUP, 0)
    listed = jnp.maximum(vert, 0).reshape(-1)
    place, at_z, at_run = listed % ROW, listed // ROW % CHIPS_Z, listed // (ROW * CHIPS_Z)
    at = (at_run // CORES * CHIPS_Z + at_z) * PARTS + at_run % CORES * ROW + place
    picked = sliced.reshape(SLICES * PARTS, SLICE_ROWS, HEAD_SIZE)[at]
    far = lax.all_gather(picked, ROW_AXES, axis=0, tiled=False)

    q = lax.all_to_all(by_head(queries, GROUP * HEAD_SIZE), HEAD_AXES, 0, 0, tiled=True)

    runs = jnp.arange(CORES, dtype=jnp.int32)
    first_blocks = ((x * CORES + runs) * CHIPS_Z + z) * ROW
    turns, tile_of, bias_of = slot_tables(vert, slash, first_blocks)
    mixed = attend_all(turns, tile_of, bias_of, q, near, far)

    returned = lax.all_to_all(mixed, HEAD_AXES, 0, 0, tiled=True)
    return returned.transpose(1, 0, 2).reshape(tokens, QUERY_HEADS * HEAD_SIZE)


def solution(mesh):
    split = Mesh(mesh.devices.reshape(CHIPS_X, CORES, CHIPS_Z, CHIPS_Y), ALL_AXES)
    rows = P(ALL_AXES, None)
    return jax.shard_map(
        shards,
        mesh=split,
        in_specs=(rows, rows, rows, P(), P()),
        out_specs=rows,
        check_vma=False,
    )
```

```python
import functools

import jax
import jax.numpy as jnp
import numpy as np
from jax import lax
from jax.experimental import pallas as pl
from jax.experimental.pallas import tpu as pltpu
from jax.sharding import Mesh, PartitionSpec as P

QUERY_HEADS = 64
KEY_VALUE_HEADS = 8
HEAD_SIZE = 128
BLOCK_TOKENS = 128
NV = 6
NS = 3
SPAN = 16

CHIPS_X, CORES, CHIPS_Z, CHIPS_Y = 4, 2, 8, 4
ALL_AXES = ("x", "c", "z", "y")
HEAD_AXES = ("c", "y")
ROW_AXES = ("x", "z")
PARTS = CORES * CHIPS_Y
GROUP = QUERY_HEADS // KEY_VALUE_HEADS
ROW = CHIPS_Y
STEPS = SPAN // ROW
WINDOW = SPAN + ROW
SLICES = CHIPS_X * CHIPS_Z
PAIR_ROWS = 2 * BLOCK_TOKENS
SLICE_ROWS = PAIR_ROWS // SLICES
PICKS = GROUP * NV
SLOTS = 1 + NS + NV
TILES = CORES * WINDOW + PICKS
HALF = CHIPS_Z // 2
FAR_X = (0, 1, -1, 2, 2)
FAR_Z = (0, 0, 0, 0, HALF)

NEG = -1e30
LOG2_SCALE = float(HEAD_SIZE**-0.5 * np.log2(np.e))


def attend_kernel(turns, tile_of, bias_of, spot, q_ref, *rest):
    near = rest[: 1 + 2 * STEPS]
    far = rest[1 + 2 * STEPS : -3]
    out_ref, tiles, sem = rest[-3:]
    head = pl.program_id(0)

    @pl.when(head == 0)
    def _():
        copies = []
        for run in range(CORES):
            first = run * WINDOW
            copies.append((near[0].at[run], tiles.at[pl.ds(first + SPAN, ROW)]))
            for step in range(STEPS):
                source = near[1 + 2 * step + run]
                at = first + SPAN - ROW * (step + 1)
                copies.append((source, tiles.at[pl.ds(at, ROW)]))
        x, z = spot[0], spot[1]
        for ref, x_back, z_back in zip(far, FAR_X, FAR_Z):
            for n in range(ref.shape[0]):
                at_x = (x - x_back + CHIPS_X) % CHIPS_X
                at_z = (z - z_back - n + CHIPS_Z) % CHIPS_Z
                first = pl.multiple_of((at_x * CHIPS_Z + at_z) * SLICE_ROWS, SLICE_ROWS)
                target = tiles.at[pl.ds(CORES * WINDOW, PICKS), pl.ds(first, SLICE_ROWS)]
                copies.append((ref.at[n], target))
        copies = [
            pltpu.make_async_copy(source, target, sem.at[n])
            for n, (source, target) in enumerate(copies)
        ]
        for copy in copies:
            copy.start()
        for copy in copies:
            copy.wait()

    rows = lax.broadcasted_iota(jnp.int32, (BLOCK_TOKENS, BLOCK_TOKENS), 0)
    cols = lax.broadcasted_iota(jnp.int32, (BLOCK_TOKENS, BLOCK_TOKENS), 1)
    causal = rows >= cols

    def attend(block, count):
        base = (head * PARTS + block) * SLOTS
        where = [tile_of[base + slot] for slot in range(count)]
        keys = jnp.concatenate([tiles[w, :BLOCK_TOKENS, :] for w in where], axis=0)
        values = jnp.concatenate([tiles[w, BLOCK_TOKENS:, :] for w in where], axis=0)
        raw = lax.dot_general(
            q_ref[block], keys, (((1,), (1,)), ((), ())), preferred_element_type=jnp.float32
        )
        scores = [raw[:, s * BLOCK_TOKENS : (s + 1) * BLOCK_TOKENS] for s in range(count)]
        scores[0] = jnp.where(causal, scores[0], NEG)
        for slot in range(1, count):
            scores[slot] = scores[slot] + bias_of[base + slot]
        best = jnp.max(functools.reduce(jnp.maximum, scores), axis=1, keepdims=True)
        weights = [jnp.exp2((s - best) * LOG2_SCALE) for s in scores]
        total = jnp.sum(functools.reduce(jnp.add, weights), axis=1, keepdims=True)
        probs = jnp.concatenate([w.astype(jnp.bfloat16) for w in weights], axis=1)
        mixed = jnp.dot(probs, values, preferred_element_type=jnp.float32)
        out_ref[block] = (mixed * (1.0 / total)).astype(jnp.bfloat16)

    for count in range(2, SLOTS + 1, 2):

        @pl.when(turns[head] == count)
        def _():
            @pl.loop(0, CORES)
            def _(run):
                for place in range(ROW):
                    attend(run * ROW + place, count)


def attend_all(turns, tile_of, bias_of, spot, q, near, far):
    head_spec = pl.BlockSpec(
        (PARTS, BLOCK_TOKENS, HEAD_SIZE), lambda head, *_: (0, 0, head)
    )
    anywhere = pl.BlockSpec(memory_space=pl.ANY)
    return pl.pallas_call(
        attend_kernel,
        out_shape=jax.ShapeDtypeStruct(q.shape, jnp.bfloat16),
        grid_spec=pltpu.PrefetchScalarGridSpec(
            num_scalar_prefetch=4,
            grid=(GROUP,),
            in_specs=[head_spec] + [anywhere] * (len(near) + len(far)),
            out_specs=head_spec,
            scratch_shapes=[
                pltpu.VMEM((TILES, PAIR_ROWS, HEAD_SIZE), jnp.bfloat16),
                pltpu.SemaphoreType.DMA((CORES * (1 + STEPS) + SLICES,)),
            ],
        ),
        compiler_params=pltpu.CompilerParams(
            dimension_semantics=("arbitrary",), vmem_limit_bytes=40 << 20
        ),
        cost_estimate=pl.CostEstimate(
            flops=4 * 64 * 6 * 128**3, bytes_accessed=10 << 20, transcendentals=64 * 6 * 128**2
        ),
        name="attend",
    )(turns, tile_of, bias_of, spot, q, *near, *far)


def split_pairs_kernel(key_ref, value_ref, out_ref):
    for head in range(KEY_VALUE_HEADS):
        columns = slice(head * HEAD_SIZE, (head + 1) * HEAD_SIZE)
        out_ref[head, :BLOCK_TOKENS, :] = key_ref[:, columns]
        out_ref[head, BLOCK_TOKENS:, :] = value_ref[:, columns]


def split_pairs(keys, values):
    return pl.pallas_call(
        split_pairs_kernel,
        out_shape=jax.ShapeDtypeStruct(
            (KEY_VALUE_HEADS, PAIR_ROWS, HEAD_SIZE), jnp.bfloat16
        ),
        cost_estimate=pl.CostEstimate(flops=0, bytes_accessed=1 << 20, transcendentals=0),
        name="split_pairs",
    )(keys, values)


def move_kernel(from_ref, to_ref):
    to_ref[...] = from_ref[...]


def split_heads(rows):
    width = rows.shape[1] // PARTS
    return pl.pallas_call(
        move_kernel,
        out_shape=jax.ShapeDtypeStruct((PARTS, BLOCK_TOKENS, width), rows.dtype),
        grid=(PARTS,),
        in_specs=[pl.BlockSpec((BLOCK_TOKENS, width), lambda n: (0, n))],
        out_specs=pl.BlockSpec((None, BLOCK_TOKENS, width), lambda n: (n, 0, 0)),
        cost_estimate=pl.CostEstimate(flops=0, bytes_accessed=4 << 20, transcendentals=0),
        name="split_heads",
    )(rows)


def merge_heads(parts):
    width = parts.shape[2]
    return pl.pallas_call(
        move_kernel,
        out_shape=jax.ShapeDtypeStruct((BLOCK_TOKENS, PARTS * width), parts.dtype),
        grid=(PARTS,),
        in_specs=[pl.BlockSpec((None, BLOCK_TOKENS, width), lambda n: (n, 0, 0))],
        out_specs=pl.BlockSpec((BLOCK_TOKENS, width), lambda n: (0, n)),
        cost_estimate=pl.CostEstimate(flops=0, bytes_accessed=4 << 20, transcendentals=0),
        name="merge_heads",
    )(parts)


def slot_tables(vert, slash, first_blocks, z):
    slash_count = jnp.sum((slash >= 1).astype(jnp.int32), axis=1)
    vert_count = jnp.sum((vert >= 0).astype(jnp.int32), axis=1)
    turns = 1 + slash_count + vert_count
    turns = (turns + 1) // 2 * 2
    part = np.arange(PARTS)
    numbers = first_blocks[part // ROW] + (part % ROW)
    own = jnp.asarray(part // ROW * WINDOW + SPAN + part % ROW, jnp.int32)
    inside = jnp.asarray(SPAN + part % ROW, jnp.int32)[None, :, None]
    inside = inside - jnp.maximum(slash, 0)[:, None, :]
    back = STEPS - inside // ROW
    run = jnp.asarray(part // ROW, jnp.int32)[None, :, None]
    held_in = jnp.where(z < back, CORES - 1 - run, run)
    near_tile = held_in * WINDOW + inside
    near_ok = (slash[:, None, :] >= 1) & (numbers[None, :, None] >= slash[:, None, :])
    far_tile = CORES * WINDOW + np.arange(PICKS, dtype=np.int32).reshape(GROUP, 1, NV)
    far_tile = jnp.broadcast_to(far_tile, (GROUP, PARTS, NV))
    hit = jnp.any(
        near_ok[:, :, :, None]
        & (
            numbers[None, :, None, None] - slash[:, None, :, None]
            == vert[:, None, None, :]
        ),
        axis=2,
    )
    far_ok = (
        (vert[:, None, :] >= 0)
        & (vert[:, None, :] < numbers[None, :, None])
        & jnp.logical_not(hit)
    )
    own_tile = jnp.broadcast_to(own[None, :, None], (GROUP, PARTS, 1))
    tile = jnp.concatenate([own_tile, near_tile, far_tile], axis=2)
    fine = jnp.concatenate([jnp.ones((GROUP, PARTS, 1), bool), near_ok, far_ok], axis=2)
    slot = np.arange(SLOTS)
    listed = jnp.concatenate(
        [jnp.ones((GROUP, 1), bool), slash >= 1, vert >= 0], axis=1
    )
    place = jnp.cumsum(listed.astype(jnp.int32), axis=1) - 1
    chosen = listed[:, :, None] & (place[:, :, None] == slot[None, None, :])
    chosen = chosen[:, None, :, :]
    tile_of = jnp.sum(jnp.where(chosen, tile[:, :, :, None], 0), axis=2)
    good = jnp.any(chosen & fine[:, :, :, None], axis=2)
    bias_of = jnp.where(good, 0.0, NEG).astype(jnp.float32)
    return turns, tile_of.reshape(-1), bias_of.reshape(-1)


def shards(queries, key_state_rows, value_state_rows, vert_blocks, slash_offsets):
    x, z = lax.axis_index("x"), lax.axis_index("z")
    key_head = lax.axis_index("c") * CHIPS_Y + lax.axis_index("y")

    def shifted(value, axis, by):
        count = lax.axis_size(axis)
        return lax.ppermute(value, axis, [(n, (n + by) % count) for n in range(count)])

    pairs = split_pairs(key_state_rows, value_state_rows)
    pairs = lax.all_to_all(pairs, HEAD_AXES, 0, 0, tiled=True)
    own = pairs.reshape(CORES, ROW, PAIR_ROWS, HEAD_SIZE)

    onward = [
        (a * CHIPS_Z + b, (a + (b + 1) // CHIPS_Z) % CHIPS_X * CHIPS_Z + (b + 1) % CHIPS_Z)
        for a in range(CHIPS_X)
        for b in range(CHIPS_Z)
    ]
    near = [own]
    first, second = own[0], own[1]
    for _ in range(STEPS):
        first = shifted(first, "z", 1)
        second = lax.ppermute(second, ROW_AXES, onward)
        near += [first, second]

    sliced = pairs.reshape(PARTS, SLICES, SLICE_ROWS, HEAD_SIZE).transpose(1, 0, 2, 3)
    sliced = lax.all_to_all(sliced, ROW_AXES, 0, 0, tiled=True)
    vert = lax.dynamic_slice_in_dim(vert_blocks, key_head * GROUP, GROUP, 0)
    slash = lax.dynamic_slice_in_dim(slash_offsets, key_head * GROUP, GROUP, 0)
    listed = jnp.maximum(vert, 0).reshape(-1)
    place, at_z, at_run = listed % ROW, listed // ROW % CHIPS_Z, listed // (ROW * CHIPS_Z)
    at = (at_run // CORES * CHIPS_Z + at_z) * PARTS + at_run % CORES * ROW + place
    picked = sliced.reshape(SLICES * PARTS, SLICE_ROWS, HEAD_SIZE)[at]

    queries = split_heads(queries)
    queries, picked = lax.optimization_barrier((queries, picked))
    q = lax.all_to_all(queries, HEAD_AXES, 0, 0, tiled=True)

    column = jnp.stack([picked] + [shifted(picked, "z", n) for n in range(1, CHIPS_Z)])
    right, left = shifted(column, "x", 1), shifted(column, "x", -1)
    far = [column, right, left]
    far += [shifted(right[:HALF], "x", 1), shifted(left[HALF:], "x", -1)]

    runs = jnp.arange(CORES, dtype=jnp.int32)
    first_blocks = ((x * CORES + runs) * CHIPS_Z + z) * ROW
    turns, tile_of, bias_of = slot_tables(vert, slash, first_blocks, z)
    spot = jnp.stack([x, z]).astype(jnp.int32)
    mixed = attend_all(turns, tile_of, bias_of, spot, q, near, far)

    returned = lax.all_to_all(mixed, HEAD_AXES, 0, 0, tiled=True)
    return merge_heads(returned)


def solution(mesh):
    split = Mesh(mesh.devices.reshape(CHIPS_X, CORES, CHIPS_Z, CHIPS_Y), ALL_AXES)
    rows = P(ALL_AXES, None)
    return jax.shard_map(
        shards,
        mesh=split,
        in_specs=(rows, rows, rows, P(), P()),
        out_specs=rows,
        check_vma=False,
    )
```

```python
import functools

import jax
import jax.numpy as jnp
import numpy as np
from jax import lax
from jax.experimental import pallas as pl
from jax.experimental.pallas import tpu as pltpu
from jax.sharding import Mesh, PartitionSpec as P

QUERY_HEADS = 64
KEY_VALUE_HEADS = 8
HEAD_SIZE = 128
BLOCK_TOKENS = 128
NV = 6
NS = 3
SPAN = 16

CHIPS_X, CORES, CHIPS_Z, CHIPS_Y = 4, 2, 8, 4
ALL_AXES = ("x", "c", "z", "y")
HEAD_AXES = ("c", "y")
ROW_AXES = ("x", "z")
PARTS = CORES * CHIPS_Y
GROUP = QUERY_HEADS // KEY_VALUE_HEADS
ROW = CHIPS_Y
STEPS = SPAN // ROW
WINDOW = SPAN + ROW
SLICES = CHIPS_X * CHIPS_Z
PAIR_ROWS = BLOCK_TOKENS + HEAD_SIZE
SLICE_ROWS = PAIR_ROWS // SLICES
PICKS = GROUP * NV
SLOTS = 1 + NS + NV
TILES = CORES * WINDOW + PICKS
HALF = CHIPS_Z // 2
FAR_X = (0, 1, -1, 2, 2)
FAR_Z = (0, 0, 0, 0, HALF)

NEG = -1e30
LOG2_SCALE = float(HEAD_SIZE**-0.5 * np.log2(np.e))


def attend_kernel(turns, tile_of, bias_of, spot, q_ref, *rest):
    near = rest[: 1 + 2 * STEPS]
    far = rest[1 + 2 * STEPS : -3]
    out_ref, tiles, sem = rest[-3:]
    head = pl.program_id(0)

    @pl.when(head == 0)
    def _():
        copies = []
        for run in range(CORES):
            first = run * WINDOW
            copies.append((near[0].at[run], tiles.at[pl.ds(first + SPAN, ROW)]))
            for step in range(STEPS):
                source = near[1 + 2 * step + run]
                at = first + SPAN - ROW * (step + 1)
                copies.append((source, tiles.at[pl.ds(at, ROW)]))
        x, z = spot[0], spot[1]
        for ref, x_back, z_back in zip(far, FAR_X, FAR_Z):
            for n in range(ref.shape[0]):
                at_x = (x - x_back + CHIPS_X) % CHIPS_X
                at_z = (z - z_back - n + CHIPS_Z) % CHIPS_Z
                first = pl.multiple_of((at_x * CHIPS_Z + at_z) * SLICE_ROWS, SLICE_ROWS)
                target = tiles.at[pl.ds(CORES * WINDOW, PICKS), pl.ds(first, SLICE_ROWS)]
                copies.append((ref.at[n], target))
        copies = [
            pltpu.make_async_copy(source, target, sem.at[n])
            for n, (source, target) in enumerate(copies)
        ]
        for copy in copies:
            copy.start()
        for copy in copies:
            copy.wait()

    rows = lax.broadcasted_iota(jnp.int32, (BLOCK_TOKENS, BLOCK_TOKENS), 0)
    cols = lax.broadcasted_iota(jnp.int32, (BLOCK_TOKENS, BLOCK_TOKENS), 1)
    causal = rows <= cols

    def attend(block, count):
        base = (head * PARTS + block) * SLOTS
        where = [tile_of[base + slot] for slot in range(count)]
        keys = jnp.concatenate([tiles[w, :BLOCK_TOKENS, :] for w in where], axis=0)
        values = jnp.concatenate([tiles[w, BLOCK_TOKENS:, :] for w in where], axis=1)
        raw = lax.dot_general(
            keys, q_ref[block], (((1,), (1,)), ((), ())), preferred_element_type=jnp.float32
        )
        scores = [raw[s * BLOCK_TOKENS : (s + 1) * BLOCK_TOKENS] for s in range(count)]
        scores[0] = jnp.where(causal, scores[0], NEG)
        for slot in range(1, count):
            scores[slot] = scores[slot] + bias_of[base + slot]
        best = jnp.max(functools.reduce(jnp.maximum, scores), axis=0, keepdims=True)
        weights = [jnp.exp2((s - best) * LOG2_SCALE) for s in scores]
        total = jnp.sum(functools.reduce(jnp.add, weights), axis=0, keepdims=True)
        probs = jnp.concatenate([w.astype(jnp.bfloat16) for w in weights], axis=0)
        mixed = jnp.dot(values, probs, preferred_element_type=jnp.float32)
        mixed = mixed * (1.0 / total)
        out_ref[block] = mixed.T.astype(jnp.bfloat16)

    for count in range(2, SLOTS + 1, 2):

        @pl.when(turns[head] == count)
        def _():
            for block in range(PARTS):
                attend(block, count)


def attend_all(turns, tile_of, bias_of, spot, q, near, far):
    head_spec = pl.BlockSpec(
        (PARTS, BLOCK_TOKENS, HEAD_SIZE), lambda head, *_: (0, 0, head)
    )
    anywhere = pl.BlockSpec(memory_space=pltpu.HBM)
    return pl.pallas_call(
        attend_kernel,
        out_shape=jax.ShapeDtypeStruct(q.shape, jnp.bfloat16),
        grid_spec=pltpu.PrefetchScalarGridSpec(
            num_scalar_prefetch=4,
            grid=(GROUP,),
            in_specs=[head_spec] + [anywhere] * (len(near) + len(far)),
            out_specs=head_spec,
            scratch_shapes=[
                pltpu.VMEM((TILES, PAIR_ROWS, HEAD_SIZE), jnp.bfloat16),
                pltpu.SemaphoreType.DMA((CORES * (1 + STEPS) + SLICES,)),
            ],
        ),
        compiler_params=pltpu.CompilerParams(
            dimension_semantics=("arbitrary",), vmem_limit_bytes=40 << 20
        ),
        cost_estimate=pl.CostEstimate(
            flops=4 * 64 * 6 * 128**3, bytes_accessed=10 << 20, transcendentals=64 * 6 * 128**2
        ),
        name="attend",
    )(turns, tile_of, bias_of, spot, q, *near, *far)


def split_pairs_kernel(key_ref, value_ref, out_ref):
    for head in range(KEY_VALUE_HEADS):
        columns = slice(head * HEAD_SIZE, (head + 1) * HEAD_SIZE)
        out_ref[head, :BLOCK_TOKENS, :] = key_ref[:, columns]
        out_ref[head, BLOCK_TOKENS:, :] = value_ref[:, columns].T


def split_pairs(keys, values):
    return pl.pallas_call(
        split_pairs_kernel,
        out_shape=jax.ShapeDtypeStruct(
            (KEY_VALUE_HEADS, PAIR_ROWS, HEAD_SIZE), jnp.bfloat16
        ),
        cost_estimate=pl.CostEstimate(flops=0, bytes_accessed=1 << 20, transcendentals=0),
        name="split_pairs",
    )(keys, values)


def move_heads_kernel(merge, from_ref, to_ref, sem):
    parts, rows = (from_ref, to_ref) if merge else (to_ref, from_ref)
    count, _, width = parts.shape
    copies = []
    for n in range(count):
        part, columns = parts.at[n], rows.at[:, pl.ds(n * width, width)]
        ends = (part, columns) if merge else (columns, part)
        copies.append(pltpu.make_async_copy(*ends, sem.at[n]))
    for copy in copies:
        copy.start()
    for copy in copies:
        copy.wait()


def move_heads(array, merge):
    wide = (BLOCK_TOKENS, array.size // BLOCK_TOKENS)
    split = (PARTS, BLOCK_TOKENS, wide[1] // PARTS)
    return pl.pallas_call(
        functools.partial(move_heads_kernel, merge),
        out_shape=jax.ShapeDtypeStruct(wide if merge else split, array.dtype),
        in_specs=[pl.BlockSpec(memory_space=pl.ANY)],
        out_specs=pl.BlockSpec(memory_space=pl.ANY),
        scratch_shapes=[pltpu.SemaphoreType.DMA((PARTS,))],
        cost_estimate=pl.CostEstimate(flops=0, bytes_accessed=4 << 20, transcendentals=0),
        name="merge_heads" if merge else "split_heads",
    )(array)


def slot_tables(vert, slash, first_blocks, z):
    slash_count = jnp.sum((slash >= 1).astype(jnp.int32), axis=1)
    vert_count = jnp.sum((vert >= 0).astype(jnp.int32), axis=1)
    turns = 1 + slash_count + vert_count
    turns = (turns + 1) // 2 * 2
    part = np.arange(PARTS)
    numbers = first_blocks[part // ROW] + (part % ROW)
    own = jnp.asarray(part // ROW * WINDOW + SPAN + part % ROW, jnp.int32)
    inside = jnp.asarray(SPAN + part % ROW, jnp.int32)[None, :, None]
    inside = inside - jnp.maximum(slash, 0)[:, None, :]
    back = STEPS - inside // ROW
    run = jnp.asarray(part // ROW, jnp.int32)[None, :, None]
    held_in = jnp.where(z < back, CORES - 1 - run, run)
    near_tile = held_in * WINDOW + inside
    near_ok = (slash[:, None, :] >= 1) & (numbers[None, :, None] >= slash[:, None, :])
    far_tile = CORES * WINDOW + np.arange(PICKS, dtype=np.int32).reshape(GROUP, 1, NV)
    far_tile = jnp.broadcast_to(far_tile, (GROUP, PARTS, NV))
    hit = jnp.any(
        near_ok[:, :, :, None]
        & (
            numbers[None, :, None, None] - slash[:, None, :, None]
            == vert[:, None, None, :]
        ),
        axis=2,
    )
    far_ok = (
        (vert[:, None, :] >= 0)
        & (vert[:, None, :] < numbers[None, :, None])
        & jnp.logical_not(hit)
    )
    own_tile = jnp.broadcast_to(own[None, :, None], (GROUP, PARTS, 1))
    tile = jnp.concatenate([own_tile, near_tile, far_tile], axis=2)
    fine = jnp.concatenate([jnp.ones((GROUP, PARTS, 1), bool), near_ok, far_ok], axis=2)
    slot = np.arange(SLOTS)
    listed = jnp.concatenate(
        [jnp.ones((GROUP, 1), bool), slash >= 1, vert >= 0], axis=1
    )
    place = jnp.cumsum(listed.astype(jnp.int32), axis=1) - 1
    chosen = listed[:, :, None] & (place[:, :, None] == slot[None, None, :])
    chosen = chosen[:, None, :, :]
    tile_of = jnp.sum(jnp.where(chosen, tile[:, :, :, None], 0), axis=2)
    good = jnp.any(chosen & fine[:, :, :, None], axis=2)
    bias_of = jnp.where(good, 0.0, NEG).astype(jnp.float32)
    return turns, tile_of.reshape(-1), bias_of.reshape(-1)


def shards(queries, key_state_rows, value_state_rows, vert_blocks, slash_offsets):
    x, z = lax.axis_index("x"), lax.axis_index("z")
    key_head = lax.axis_index("c") * CHIPS_Y + lax.axis_index("y")

    def shifted(value, axis, by):
        count = lax.axis_size(axis)
        return lax.ppermute(value, axis, [(n, (n + by) % count) for n in range(count)])

    pairs = split_pairs(key_state_rows, value_state_rows)
    pairs = lax.all_to_all(pairs, HEAD_AXES, 0, 0, tiled=True)
    own = pairs.reshape(CORES, ROW, PAIR_ROWS, HEAD_SIZE)

    onward = [
        (a * CHIPS_Z + b, (a + (b + 1) // CHIPS_Z) % CHIPS_X * CHIPS_Z + (b + 1) % CHIPS_Z)
        for a in range(CHIPS_X)
        for b in range(CHIPS_Z)
    ]
    def passed_on(first, second):
        return shifted(first, "z", 1), lax.ppermute(second, ROW_AXES, onward)

    sliced = pairs.reshape(PARTS, SLICES, SLICE_ROWS, HEAD_SIZE).transpose(1, 0, 2, 3)
    sliced = lax.all_to_all(sliced, ROW_AXES, 0, 0, tiled=True)
    one = passed_on(own[0], own[1])
    two = passed_on(*one)
    sliced, two = lax.optimization_barrier((sliced, two))
    vert = lax.dynamic_slice_in_dim(vert_blocks, key_head * GROUP, GROUP, 0)
    slash = lax.dynamic_slice_in_dim(slash_offsets, key_head * GROUP, GROUP, 0)
    listed = jnp.maximum(vert, 0).reshape(-1)
    place, at_z, at_run = listed % ROW, listed // ROW % CHIPS_Z, listed // (ROW * CHIPS_Z)
    at = (at_run // CORES * CHIPS_Z + at_z) * PARTS + at_run % CORES * ROW + place
    picked = sliced.reshape(SLICES * PARTS, SLICE_ROWS, HEAD_SIZE)[at]

    queries = move_heads(queries, False)
    queries, picked = lax.optimization_barrier((queries, picked))
    q = lax.all_to_all(queries, HEAD_AXES, 0, 0, tiled=True)

    three = passed_on(*two)
    ahead, behind = [], []
    for n in range(HALF):
        behind += [shifted(behind[-1] if n else picked, "z", 1)]
        if n < HALF - 1:
            ahead += [shifted(ahead[-1] if n else picked, "z", -1)]
    column = [picked] + behind + ahead[::-1]
    column, three = lax.optimization_barrier((column, three))
    column = jnp.stack(column)
    four = passed_on(*three)
    right, left = shifted(column, "x", 1), shifted(column, "x", -1)
    far = [column, right, left]
    far += [shifted(right[:HALF], "x", 1), shifted(left[HALF:], "x", -1)]
    near = [own, *one, *two, *three, *four]

    runs = jnp.arange(CORES, dtype=jnp.int32)
    first_blocks = ((x * CORES + runs) * CHIPS_Z + z) * ROW
    turns, tile_of, bias_of = slot_tables(vert, slash, first_blocks, z)
    spot = jnp.stack([x, z]).astype(jnp.int32)
    mixed = attend_all(turns, tile_of, bias_of, spot, q, near, far)

    returned = lax.all_to_all(mixed, HEAD_AXES, 0, 0, tiled=True)
    return move_heads(returned, True)


def solution(mesh):
    split = Mesh(mesh.devices.reshape(CHIPS_X, CORES, CHIPS_Z, CHIPS_Y), ALL_AXES)
    rows = P(ALL_AXES, None)
    return jax.shard_map(
        shards,
        mesh=split,
        in_specs=(rows, rows, rows, P(), P()),
        out_specs=rows,
        check_vma=False,
    )
```

```python
import functools

import jax
import jax.numpy as jnp
import numpy as np
from jax import lax
from jax.experimental import pallas as pl
from jax.experimental.pallas import tpu as pltpu
from jax.sharding import Mesh, PartitionSpec as P

QUERY_HEADS = 64
KEY_VALUE_HEADS = 8
HEAD_SIZE = 128
BLOCK_TOKENS = 128
NV = 6
NS = 3
SPAN = 16

CHIPS_X, CORES, CHIPS_Z, CHIPS_Y = 4, 2, 8, 4
ALL_AXES = ("x", "c", "z", "y")
HEAD_AXES = ("c", "y")
ROW_AXES = ("x", "z")
PARTS = CORES * CHIPS_Y
GROUP = QUERY_HEADS // KEY_VALUE_HEADS
ROW = CHIPS_Y
STEPS = SPAN // ROW
WINDOW = SPAN + ROW
SLICES = CHIPS_X * CHIPS_Z
PAIR_ROWS = BLOCK_TOKENS + HEAD_SIZE
SLICE_ROWS = PAIR_ROWS // SLICES
PICKS = GROUP * NV
SLOTS = 1 + NS + NV
TILES = CORES * WINDOW + PICKS
HALF = CHIPS_Z // 2
FAR_X = (0, 0, 1, 1, -1, -1, 2, 2)
FAR_Z = (0, HALF, 0, HALF, 0, HALF, 0, HALF)

NEG = -1e30
LOG2_SCALE = float(HEAD_SIZE**-0.5 * np.log2(np.e))


def attend_kernel(turns, tile_of, bias_of, spot, q_ref, *rest):
    near = rest[: 1 + 2 * STEPS]
    far = rest[1 + 2 * STEPS : -3]
    out_ref, tiles, sem = rest[-3:]
    head = pl.program_id(0)

    @pl.when(head == 0)
    def _():
        copies = []
        for run in range(CORES):
            first = run * WINDOW
            copies.append((near[0].at[run], tiles.at[pl.ds(first + SPAN, ROW)]))
            for step in range(STEPS):
                source = near[1 + 2 * step + run]
                at = first + SPAN - ROW * (step + 1)
                copies.append((source, tiles.at[pl.ds(at, ROW)]))
        x, z = spot[0], spot[1]
        for ref, x_back, z_back in zip(far, FAR_X, FAR_Z):
            for n in range(ref.shape[0]):
                at_x = (x - x_back + CHIPS_X) % CHIPS_X
                at_z = (z - z_back - n + CHIPS_Z) % CHIPS_Z
                first = pl.multiple_of((at_x * CHIPS_Z + at_z) * SLICE_ROWS, SLICE_ROWS)
                target = tiles.at[pl.ds(CORES * WINDOW, PICKS), pl.ds(first, SLICE_ROWS)]
                copies.append((ref.at[n], target))
        copies = [
            pltpu.make_async_copy(source, target, sem.at[n])
            for n, (source, target) in enumerate(copies)
        ]
        for copy in copies:
            copy.start()
        for copy in copies:
            copy.wait()

    rows = lax.broadcasted_iota(jnp.int32, (BLOCK_TOKENS, BLOCK_TOKENS), 0)
    cols = lax.broadcasted_iota(jnp.int32, (BLOCK_TOKENS, BLOCK_TOKENS), 1)
    causal = rows <= cols

    def attend(block, count):
        base = (head * PARTS + block) * SLOTS
        where = [tile_of[base + slot] for slot in range(count)]
        keys = jnp.concatenate([tiles[w, :BLOCK_TOKENS, :] for w in where], axis=0)
        values = jnp.concatenate([tiles[w, BLOCK_TOKENS:, :] for w in where], axis=1)
        raw = lax.dot_general(
            keys, q_ref[block], (((1,), (1,)), ((), ())), preferred_element_type=jnp.float32
        )
        scores = [raw[s * BLOCK_TOKENS : (s + 1) * BLOCK_TOKENS] for s in range(count)]
        scores[0] = jnp.where(causal, scores[0], NEG)
        for slot in range(1, count):
            scores[slot] = scores[slot] + bias_of[base + slot]
        best = jnp.max(functools.reduce(jnp.maximum, scores), axis=0, keepdims=True)
        weights = [jnp.exp2((s - best) * LOG2_SCALE) for s in scores]
        total = jnp.sum(functools.reduce(jnp.add, weights), axis=0, keepdims=True)
        probs = jnp.concatenate([w.astype(jnp.bfloat16) for w in weights], axis=0)
        mixed = jnp.dot(values, probs, preferred_element_type=jnp.float32)
        mixed = mixed * (1.0 / total)
        out_ref[block] = mixed.T.astype(jnp.bfloat16)

    for count in range(2, SLOTS + 1, 2):

        @pl.when(turns[head] == count)
        def _():
            for block in range(PARTS):
                attend(block, count)


def attend_all(turns, tile_of, bias_of, spot, q, near, far):
    head_spec = pl.BlockSpec(
        (PARTS, BLOCK_TOKENS, HEAD_SIZE), lambda head, *_: (0, 0, head)
    )
    anywhere = pl.BlockSpec(memory_space=pltpu.HBM)
    return pl.pallas_call(
        attend_kernel,
        out_shape=jax.ShapeDtypeStruct(q.shape, jnp.bfloat16),
        grid_spec=pltpu.PrefetchScalarGridSpec(
            num_scalar_prefetch=4,
            grid=(GROUP,),
            in_specs=[head_spec] + [anywhere] * (len(near) + len(far)),
            out_specs=head_spec,
            scratch_shapes=[
                pltpu.VMEM((TILES, PAIR_ROWS, HEAD_SIZE), jnp.bfloat16),
                pltpu.SemaphoreType.DMA((CORES * (1 + STEPS) + SLICES,)),
            ],
        ),
        compiler_params=pltpu.CompilerParams(
            dimension_semantics=("arbitrary",), vmem_limit_bytes=60 << 20
        ),
        cost_estimate=pl.CostEstimate(
            flops=4 * 64 * 6 * 128**3, bytes_accessed=10 << 20, transcendentals=64 * 6 * 128**2
        ),
        name="attend",
    )(turns, tile_of, bias_of, spot, q, *near, *far)


def split_pairs_kernel(key_ref, value_ref, out_ref):
    for head in range(KEY_VALUE_HEADS):
        columns = slice(head * HEAD_SIZE, (head + 1) * HEAD_SIZE)
        out_ref[head, :BLOCK_TOKENS, :] = key_ref[:, columns]
        out_ref[head, BLOCK_TOKENS:, :] = value_ref[:, columns].T


def split_pairs(keys, values):
    return pl.pallas_call(
        split_pairs_kernel,
        out_shape=jax.ShapeDtypeStruct(
            (KEY_VALUE_HEADS, PAIR_ROWS, HEAD_SIZE), jnp.bfloat16
        ),
        cost_estimate=pl.CostEstimate(flops=0, bytes_accessed=1 << 20, transcendentals=0),
        compiler_params=pltpu.CompilerParams(vmem_limit_bytes=8 << 20),
        name="split_pairs",
    )(keys, values)


def move_heads_kernel(merge, from_ref, to_ref, sem):
    parts, rows = (from_ref, to_ref) if merge else (to_ref, from_ref)
    count, _, width = parts.shape
    copies = []
    for n in range(count):
        part, columns = parts.at[n], rows.at[:, pl.ds(n * width, width)]
        ends = (part, columns) if merge else (columns, part)
        copies.append(pltpu.make_async_copy(*ends, sem.at[n]))
    for copy in copies:
        copy.start()
    for copy in copies:
        copy.wait()


def move_heads(array, merge):
    wide = (BLOCK_TOKENS, array.size // BLOCK_TOKENS)
    split = (PARTS, BLOCK_TOKENS, wide[1] // PARTS)
    return pl.pallas_call(
        functools.partial(move_heads_kernel, merge),
        out_shape=jax.ShapeDtypeStruct(wide if merge else split, array.dtype),
        in_specs=[pl.BlockSpec(memory_space=pltpu.VMEM if merge else pltpu.HBM)],
        out_specs=pl.BlockSpec(memory_space=pltpu.HBM if merge else pltpu.VMEM),
        scratch_shapes=[pltpu.SemaphoreType.DMA((PARTS,))],
        cost_estimate=pl.CostEstimate(flops=0, bytes_accessed=4 << 20, transcendentals=0),
        compiler_params=pltpu.CompilerParams(vmem_limit_bytes=8 << 20),
        name="merge_heads" if merge else "split_heads",
    )(array)


def stack_kernel(*refs):
    halves = refs[CHIPS_Z:]
    for n, ref in enumerate(refs[:CHIPS_Z]):
        halves[n // HALF][n % HALF] = ref[...]


def stack_halves(parts):
    half = jax.ShapeDtypeStruct((HALF, *parts[0].shape), parts[0].dtype)
    return pl.pallas_call(
        stack_kernel,
        out_shape=(half, half),
        cost_estimate=pl.CostEstimate(flops=0, bytes_accessed=2 << 20, transcendentals=0),
        compiler_params=pltpu.CompilerParams(vmem_limit_bytes=8 << 20),
        name="stack_halves",
    )(*parts)


def slot_tables(vert, slash, first_blocks, z):
    slash_count = jnp.sum((slash >= 1).astype(jnp.int32), axis=1)
    vert_count = jnp.sum((vert >= 0).astype(jnp.int32), axis=1)
    turns = 1 + slash_count + vert_count
    turns = (turns + 1) // 2 * 2
    part = np.arange(PARTS)
    numbers = first_blocks[part // ROW] + (part % ROW)
    own = jnp.asarray(part // ROW * WINDOW + SPAN + part % ROW, jnp.int32)
    inside = jnp.asarray(SPAN + part % ROW, jnp.int32)[None, :, None]
    inside = inside - jnp.maximum(slash, 0)[:, None, :]
    back = STEPS - inside // ROW
    run = jnp.asarray(part // ROW, jnp.int32)[None, :, None]
    held_in = jnp.where(z < back, CORES - 1 - run, run)
    near_tile = held_in * WINDOW + inside
    near_ok = (slash[:, None, :] >= 1) & (numbers[None, :, None] >= slash[:, None, :])
    far_tile = CORES * WINDOW + np.arange(PICKS, dtype=np.int32).reshape(GROUP, 1, NV)
    far_tile = jnp.broadcast_to(far_tile, (GROUP, PARTS, NV))
    hit = jnp.any(
        near_ok[:, :, :, None]
        & (
            numbers[None, :, None, None] - slash[:, None, :, None]
            == vert[:, None, None, :]
        ),
        axis=2,
    )
    far_ok = (
        (vert[:, None, :] >= 0)
        & (vert[:, None, :] < numbers[None, :, None])
        & jnp.logical_not(hit)
    )
    own_tile = jnp.broadcast_to(own[None, :, None], (GROUP, PARTS, 1))
    tile = jnp.concatenate([own_tile, near_tile, far_tile], axis=2)
    fine = jnp.concatenate([jnp.ones((GROUP, PARTS, 1), bool), near_ok, far_ok], axis=2)
    slot = np.arange(SLOTS)
    listed = jnp.concatenate(
        [jnp.ones((GROUP, 1), bool), slash >= 1, vert >= 0], axis=1
    )
    place = jnp.cumsum(listed.astype(jnp.int32), axis=1) - 1
    chosen = listed[:, :, None] & (place[:, :, None] == slot[None, None, :])
    chosen = chosen[:, None, :, :]
    tile_of = jnp.sum(jnp.where(chosen, tile[:, :, :, None], 0), axis=2)
    good = jnp.any(chosen & fine[:, :, :, None], axis=2)
    bias_of = jnp.where(good, 0.0, NEG).astype(jnp.float32)
    return turns, tile_of.reshape(-1), bias_of.reshape(-1)


def shards(queries, key_state_rows, value_state_rows, vert_blocks, slash_offsets):
    x, z = lax.axis_index("x"), lax.axis_index("z")
    key_head = lax.axis_index("c") * CHIPS_Y + lax.axis_index("y")

    def shifted(value, axis, by):
        count = lax.axis_size(axis)
        return lax.ppermute(value, axis, [(n, (n + by) % count) for n in range(count)])

    pairs = split_pairs(key_state_rows, value_state_rows)
    pairs = lax.all_to_all(pairs, HEAD_AXES, 0, 0, tiled=True)
    own = pairs.reshape(CORES, ROW, PAIR_ROWS, HEAD_SIZE)

    onward = [
        (a * CHIPS_Z + b, (a + (b + 1) // CHIPS_Z) % CHIPS_X * CHIPS_Z + (b + 1) % CHIPS_Z)
        for a in range(CHIPS_X)
        for b in range(CHIPS_Z)
    ]
    def passed_on(first, second):
        return shifted(first, "z", 1), lax.ppermute(second, ROW_AXES, onward)

    sliced = pairs.reshape(PARTS, SLICES, SLICE_ROWS, HEAD_SIZE).transpose(1, 0, 2, 3)
    sliced = lax.all_to_all(sliced, ROW_AXES, 0, 0, tiled=True)
    one = passed_on(own[0], own[1])
    two = passed_on(*one)
    vert = lax.dynamic_slice_in_dim(vert_blocks, key_head * GROUP, GROUP, 0)
    slash = lax.dynamic_slice_in_dim(slash_offsets, key_head * GROUP, GROUP, 0)
    listed = jnp.maximum(vert, 0).reshape(-1)
    place, at_z, at_run = listed % ROW, listed // ROW % CHIPS_Z, listed // (ROW * CHIPS_Z)
    at = (at_run // CORES * CHIPS_Z + at_z) * PARTS + at_run % CORES * ROW + place
    picked = sliced.reshape(SLICES * PARTS, SLICE_ROWS, HEAD_SIZE)[at]

    queries = move_heads(queries, False)
    queries, picked = lax.optimization_barrier((queries, picked))
    q = lax.all_to_all(queries, HEAD_AXES, 0, 0, tiled=True)

    ahead, behind = [], []
    for n in range(HALF):
        behind += [shifted(behind[-1] if n else picked, "z", 1)]
        if n < HALF - 1:
            ahead += [shifted(ahead[-1] if n else picked, "z", -1)]
    column = [picked] + behind + ahead[::-1]
    column, two = lax.optimization_barrier((column, two))
    lower, upper = stack_halves(column)
    three = passed_on(*two)
    four = passed_on(*three)
    right, left = shifted(lower, "x", 1), shifted(upper, "x", -1)
    far = [lower, upper, right, shifted(upper, "x", 1), shifted(lower, "x", -1), left]
    far += [shifted(right, "x", 1), shifted(left, "x", -1)]
    near = [own, *one, *two, *three, *four]

    runs = jnp.arange(CORES, dtype=jnp.int32)
    first_blocks = ((x * CORES + runs) * CHIPS_Z + z) * ROW
    turns, tile_of, bias_of = slot_tables(vert, slash, first_blocks, z)
    spot = jnp.stack([x, z]).astype(jnp.int32)
    mixed = attend_all(turns, tile_of, bias_of, spot, q, near, far)

    returned = lax.all_to_all(mixed, HEAD_AXES, 0, 0, tiled=True)
    return move_heads(returned, True)


def solution(mesh):
    split = Mesh(mesh.devices.reshape(CHIPS_X, CORES, CHIPS_Z, CHIPS_Y), ALL_AXES)
    rows = P(ALL_AXES, None)
    return jax.shard_map(
        shards,
        mesh=split,
        in_specs=(rows, rows, rows, P(), P()),
        out_specs=rows,
        check_vma=False,
    )
```

```python
import functools

import jax
import jax.numpy as jnp
import numpy as np
from jax import lax
from jax.experimental import pallas as pl
from jax.experimental.pallas import tpu as pltpu
from jax.sharding import Mesh, PartitionSpec as P

QUERY_HEADS = 64
KEY_VALUE_HEADS = 8
HEAD_SIZE = 128
BLOCK_TOKENS = 128
NV = 6
NS = 3
SPAN = 16

CHIPS_X, CORES, CHIPS_Z, CHIPS_Y = 4, 2, 8, 4
ALL_AXES = ("x", "c", "z", "y")
HEAD_AXES = ("c", "y")
ROW_AXES = ("x", "z")
PARTS = CORES * CHIPS_Y
GROUP = QUERY_HEADS // KEY_VALUE_HEADS
ROW = CHIPS_Y
STEPS = SPAN // ROW
WINDOW = SPAN + ROW
SLICES = CHIPS_X * CHIPS_Z
PAIR_ROWS = BLOCK_TOKENS + HEAD_SIZE
SLICE_ROWS = PAIR_ROWS // SLICES
PICKS = GROUP * NV
SLOTS = 1 + NS + NV
CALLS = 2
HEADS_A_CALL = GROUP // CALLS
TILES = CORES * WINDOW + HEADS_A_CALL * NV
COUNTS = (4, 6, SLOTS)
HALF = CHIPS_Z // 2
FAR_X = (0, 0, 1, 1, -1, -1, 2, 2)
FAR_Z = (0, HALF, 0, HALF, 0, HALF, 0, HALF)

NEG = -1e30
LOG2_SCALE = float(HEAD_SIZE**-0.5 * np.log2(np.e))


def attend_kernel(half, turns, tile_of, bias_of, spot, q_ref, *rest):
    near = rest[: 1 + 2 * STEPS]
    far = rest[1 + 2 * STEPS : -3]
    out_ref, tiles, sem = rest[-3:]
    head = pl.program_id(0) + half * HEADS_A_CALL

    @pl.when(pl.program_id(0) == 0)
    def _():
        copies = []
        for run in range(CORES):
            first = run * WINDOW
            copies.append((near[0].at[run], tiles.at[pl.ds(first + SPAN, ROW)]))
            for step in range(STEPS):
                source = near[1 + 2 * step + run]
                at = first + SPAN - ROW * (step + 1)
                copies.append((source, tiles.at[pl.ds(at, ROW)]))
        x, z = spot[0], spot[1]
        for ref, x_back, z_back in zip(far, FAR_X, FAR_Z):
            for n in range(ref.shape[0]):
                at_x = (x - x_back + CHIPS_X) % CHIPS_X
                at_z = (z - z_back - n + CHIPS_Z) % CHIPS_Z
                first = pl.multiple_of((at_x * CHIPS_Z + at_z) * SLICE_ROWS, SLICE_ROWS)
                count = HEADS_A_CALL * NV
                target = tiles.at[pl.ds(CORES * WINDOW, count), pl.ds(first, SLICE_ROWS)]
                copies.append((ref.at[n, pl.ds(half * count, count)], target))
        copies = [
            pltpu.make_async_copy(source, target, sem.at[n])
            for n, (source, target) in enumerate(copies)
        ]
        for copy in copies:
            copy.start()
        for copy in copies:
            copy.wait()

    rows = lax.broadcasted_iota(jnp.int32, (BLOCK_TOKENS, BLOCK_TOKENS), 0)
    cols = lax.broadcasted_iota(jnp.int32, (BLOCK_TOKENS, BLOCK_TOKENS), 1)
    causal = rows <= cols

    def attend(block, count):
        base = (head * PARTS + block) * SLOTS
        where = [tile_of[base + slot] for slot in range(count)]
        keys = jnp.concatenate([tiles[w, :BLOCK_TOKENS, :] for w in where], axis=0)
        values = jnp.concatenate([tiles[w, BLOCK_TOKENS:, :] for w in where], axis=1)
        raw = lax.dot_general(
            keys, q_ref[block], (((1,), (1,)), ((), ())), preferred_element_type=jnp.float32
        )
        scores = [raw[s * BLOCK_TOKENS : (s + 1) * BLOCK_TOKENS] for s in range(count)]
        scores[0] = jnp.where(causal, scores[0], NEG)
        for slot in range(1, count):
            scores[slot] = scores[slot] + bias_of[base + slot]
        best = jnp.max(functools.reduce(jnp.maximum, scores), axis=0, keepdims=True)
        weights = [jnp.exp2((s - best) * LOG2_SCALE) for s in scores]
        total = jnp.sum(functools.reduce(jnp.add, weights), axis=0, keepdims=True)
        probs = jnp.concatenate([w.astype(jnp.bfloat16) for w in weights], axis=0)
        mixed = jnp.dot(values, probs, preferred_element_type=jnp.float32)
        mixed = mixed * (1.0 / total)
        out_ref[block] = mixed.T.astype(jnp.bfloat16)

    for count in COUNTS:

        @pl.when(turns[head] == count)
        def _():
            for block in range(PARTS):
                attend(block, count)


def attend_half(half, turns, tile_of, bias_of, spot, q, near, far):
    block = (PARTS, BLOCK_TOKENS, HEAD_SIZE)
    width = HEADS_A_CALL * HEAD_SIZE
    anywhere = pl.BlockSpec(memory_space=pltpu.HBM)
    return pl.pallas_call(
        functools.partial(attend_kernel, half),
        out_shape=jax.ShapeDtypeStruct((PARTS, BLOCK_TOKENS, width), jnp.bfloat16),
        grid_spec=pltpu.PrefetchScalarGridSpec(
            num_scalar_prefetch=4,
            grid=(HEADS_A_CALL,),
            in_specs=[
                pl.BlockSpec(block, lambda head, *_: (0, 0, head + half * HEADS_A_CALL))
            ]
            + [anywhere] * (len(near) + len(far)),
            out_specs=pl.BlockSpec(block, lambda head, *_: (0, 0, head)),
            scratch_shapes=[
                pltpu.VMEM((TILES, PAIR_ROWS, HEAD_SIZE), jnp.bfloat16),
                pltpu.SemaphoreType.DMA((CORES * (1 + STEPS) + SLICES,)),
            ],
        ),
        compiler_params=pltpu.CompilerParams(
            dimension_semantics=("arbitrary",), vmem_limit_bytes=60 << 20
        ),
        cost_estimate=pl.CostEstimate(
            flops=4 * 32 * 6 * 128**3, bytes_accessed=8 << 20, transcendentals=32 * 6 * 128**2
        ),
        name="attend",
    )(turns, tile_of, bias_of, spot, q, *near, *far)


def split_pairs_kernel(key_ref, value_ref, out_ref):
    for head in range(KEY_VALUE_HEADS):
        columns = slice(head * HEAD_SIZE, (head + 1) * HEAD_SIZE)
        out_ref[head, :BLOCK_TOKENS, :] = key_ref[:, columns]
        out_ref[head, BLOCK_TOKENS:, :] = value_ref[:, columns].T


def split_pairs(keys, values):
    return pl.pallas_call(
        split_pairs_kernel,
        out_shape=jax.ShapeDtypeStruct(
            (KEY_VALUE_HEADS, PAIR_ROWS, HEAD_SIZE), jnp.bfloat16
        ),
        cost_estimate=pl.CostEstimate(flops=0, bytes_accessed=1 << 20, transcendentals=0),
        compiler_params=pltpu.CompilerParams(vmem_limit_bytes=8 << 20),
        name="split_pairs",
    )(keys, values)


def split_heads_kernel(rows, parts, sem):
    width = parts.shape[2]
    copies = [
        pltpu.make_async_copy(rows.at[:, pl.ds(n * width, width)], parts.at[n], sem.at[n])
        for n in range(PARTS)
    ]
    for copy in copies:
        copy.start()
    for copy in copies:
        copy.wait()


def split_heads(rows):
    return pl.pallas_call(
        split_heads_kernel,
        out_shape=jax.ShapeDtypeStruct(
            (PARTS, BLOCK_TOKENS, rows.shape[1] // PARTS), rows.dtype
        ),
        in_specs=[pl.BlockSpec(memory_space=pltpu.HBM)],
        out_specs=pl.BlockSpec(memory_space=pltpu.VMEM),
        scratch_shapes=[pltpu.SemaphoreType.DMA((PARTS,))],
        cost_estimate=pl.CostEstimate(flops=0, bytes_accessed=4 << 20, transcendentals=0),
        compiler_params=pltpu.CompilerParams(vmem_limit_bytes=8 << 20),
        name="split_heads",
    )(rows)


def merge_heads_kernel(*refs):
    halves, rows, sem = refs[:CALLS], refs[CALLS], refs[CALLS + 1]
    width = halves[0].shape[2]
    copies = []
    for n in range(PARTS):
        for half, parts in enumerate(halves):
            place = n * CALLS + half
            columns = rows.at[:, pl.ds(place * width, width)]
            copies.append(pltpu.make_async_copy(parts.at[n], columns, sem.at[place]))
    for copy in copies:
        copy.start()
    for copy in copies:
        copy.wait()


def merge_heads(*halves):
    return pl.pallas_call(
        merge_heads_kernel,
        out_shape=jax.ShapeDtypeStruct(
            (BLOCK_TOKENS, QUERY_HEADS * HEAD_SIZE), halves[0].dtype
        ),
        in_specs=[pl.BlockSpec(memory_space=pltpu.VMEM)] * CALLS,
        out_specs=pl.BlockSpec(memory_space=pltpu.HBM),
        scratch_shapes=[pltpu.SemaphoreType.DMA((PARTS * CALLS,))],
        cost_estimate=pl.CostEstimate(flops=0, bytes_accessed=4 << 20, transcendentals=0),
        compiler_params=pltpu.CompilerParams(vmem_limit_bytes=8 << 20),
        name="merge_heads",
    )(*halves)


def stack_kernel(*refs):
    halves = refs[CHIPS_Z:]
    for n, ref in enumerate(refs[:CHIPS_Z]):
        halves[n // HALF][n % HALF] = ref[...]


def stack_halves(parts):
    half = jax.ShapeDtypeStruct((HALF, *parts[0].shape), parts[0].dtype)
    return pl.pallas_call(
        stack_kernel,
        out_shape=(half, half),
        cost_estimate=pl.CostEstimate(flops=0, bytes_accessed=2 << 20, transcendentals=0),
        compiler_params=pltpu.CompilerParams(vmem_limit_bytes=8 << 20),
        name="stack_halves",
    )(*parts)


def slot_tables(vert, slash, first_blocks, z):
    slash_count = jnp.sum((slash >= 1).astype(jnp.int32), axis=1)
    vert_count = jnp.sum((vert >= 0).astype(jnp.int32), axis=1)
    turns = 1 + slash_count + vert_count
    turns = sum(
        jnp.where(turns > low, high - low, 0) for low, high in zip((0, *COUNTS), COUNTS)
    )
    part = np.arange(PARTS)
    numbers = first_blocks[part // ROW] + (part % ROW)
    own = jnp.asarray(part // ROW * WINDOW + SPAN + part % ROW, jnp.int32)
    inside = jnp.asarray(SPAN + part % ROW, jnp.int32)[None, :, None]
    inside = inside - jnp.maximum(slash, 0)[:, None, :]
    back = STEPS - inside // ROW
    run = jnp.asarray(part // ROW, jnp.int32)[None, :, None]
    held_in = jnp.where(z < back, CORES - 1 - run, run)
    near_tile = held_in * WINDOW + inside
    near_ok = (slash[:, None, :] >= 1) & (numbers[None, :, None] >= slash[:, None, :])
    far_tile = np.arange(PICKS, dtype=np.int32).reshape(GROUP, 1, NV) % (HEADS_A_CALL * NV)
    far_tile = CORES * WINDOW + far_tile
    far_tile = jnp.broadcast_to(far_tile, (GROUP, PARTS, NV))
    hit = jnp.any(
        near_ok[:, :, :, None]
        & (
            numbers[None, :, None, None] - slash[:, None, :, None]
            == vert[:, None, None, :]
        ),
        axis=2,
    )
    far_ok = (
        (vert[:, None, :] >= 0)
        & (vert[:, None, :] < numbers[None, :, None])
        & jnp.logical_not(hit)
    )
    own_tile = jnp.broadcast_to(own[None, :, None], (GROUP, PARTS, 1))
    tile = jnp.concatenate([own_tile, near_tile, far_tile], axis=2)
    fine = jnp.concatenate([jnp.ones((GROUP, PARTS, 1), bool), near_ok, far_ok], axis=2)
    slot = np.arange(SLOTS)
    listed = jnp.concatenate(
        [jnp.ones((GROUP, 1), bool), slash >= 1, vert >= 0], axis=1
    )
    place = jnp.cumsum(listed.astype(jnp.int32), axis=1) - 1
    chosen = listed[:, :, None] & (place[:, :, None] == slot[None, None, :])
    chosen = chosen[:, None, :, :]
    tile_of = jnp.sum(jnp.where(chosen, tile[:, :, :, None], 0), axis=2)
    good = jnp.any(chosen & fine[:, :, :, None], axis=2)
    bias_of = jnp.where(good, 0.0, NEG).astype(jnp.float32)
    return turns, tile_of.reshape(-1), bias_of.reshape(-1)


def shards(queries, key_state_rows, value_state_rows, vert_blocks, slash_offsets):
    x, z = lax.axis_index("x"), lax.axis_index("z")
    key_head = lax.axis_index("c") * CHIPS_Y + lax.axis_index("y")

    def shifted(value, axis, by):
        count = lax.axis_size(axis)
        return lax.ppermute(value, axis, [(n, (n + by) % count) for n in range(count)])

    pairs = split_pairs(key_state_rows, value_state_rows)
    pairs = lax.all_to_all(pairs, HEAD_AXES, 0, 0, tiled=True)
    own = pairs.reshape(CORES, ROW, PAIR_ROWS, HEAD_SIZE)

    onward = [
        (a * CHIPS_Z + b, (a + (b + 1) // CHIPS_Z) % CHIPS_X * CHIPS_Z + (b + 1) % CHIPS_Z)
        for a in range(CHIPS_X)
        for b in range(CHIPS_Z)
    ]
    def passed_on(first, second):
        return shifted(first, "z", 1), lax.ppermute(second, ROW_AXES, onward)

    sliced = pairs.reshape(PARTS, SLICES, SLICE_ROWS, HEAD_SIZE).transpose(1, 0, 2, 3)
    sliced = lax.all_to_all(sliced, ROW_AXES, 0, 0, tiled=True)
    vert = lax.dynamic_slice_in_dim(vert_blocks, key_head * GROUP, GROUP, 0)
    slash = lax.dynamic_slice_in_dim(slash_offsets, key_head * GROUP, GROUP, 0)
    listed = jnp.maximum(vert, 0).reshape(-1)
    place, at_z, at_run = listed % ROW, listed // ROW % CHIPS_Z, listed // (ROW * CHIPS_Z)
    at = (at_run // CORES * CHIPS_Z + at_z) * PARTS + at_run % CORES * ROW + place
    picked = sliced.reshape(SLICES * PARTS, SLICE_ROWS, HEAD_SIZE)[at]

    queries = split_heads(queries)
    q = lax.all_to_all(queries, HEAD_AXES, 0, 0, tiled=True)

    behind = shifted(picked, "z", 1)
    ahead = [picked]
    for _ in range(CHIPS_Z - 2):
        ahead += [shifted(ahead[-1], "z", -1)]
    column = [picked, behind] + ahead[:0:-1]
    first, second, behind = lax.optimization_barrier((own[0], own[1], behind))
    one = passed_on(first, second)
    two = passed_on(*one)
    column, two = lax.optimization_barrier((column, two))
    lower, upper = stack_halves(column)
    three = passed_on(*two)
    four = passed_on(*three)
    right, left = shifted(lower, "x", 1), shifted(upper, "x", -1)
    far = [lower, upper, right, shifted(upper, "x", 1), shifted(lower, "x", -1), left]
    far += [shifted(right, "x", 1), shifted(left, "x", -1)]
    near = [own, *one, *two, *three, *four]

    runs = jnp.arange(CORES, dtype=jnp.int32)
    first_blocks = ((x * CORES + runs) * CHIPS_Z + z) * ROW
    turns, tile_of, bias_of = slot_tables(vert, slash, first_blocks, z)
    spot = jnp.stack([x, z]).astype(jnp.int32)
    returned = []
    for half in range(CALLS):
        mixed = attend_half(half, turns, tile_of, bias_of, spot, q, near, far)
        returned += [lax.all_to_all(mixed, HEAD_AXES, 0, 0, tiled=True)]
    return merge_heads(*returned)


def solution(mesh):
    split = Mesh(mesh.devices.reshape(CHIPS_X, CORES, CHIPS_Z, CHIPS_Y), ALL_AXES)
    rows = P(ALL_AXES, None)
    return jax.shard_map(
        shards,
        mesh=split,
        in_specs=(rows, rows, rows, P(), P()),
        out_specs=rows,
        check_vma=False,
    )
```

```python
import functools

import jax
import jax.numpy as jnp
import numpy as np
from jax import lax
from jax.experimental import pallas as pl
from jax.experimental.pallas import tpu as pltpu
from jax.sharding import Mesh, PartitionSpec as P

QUERY_HEADS = 64
KEY_VALUE_HEADS = 8
HEAD_SIZE = 128
BLOCK_TOKENS = 128
NV = 6
NS = 3
SPAN = 16

CHIPS_X, CORES, CHIPS_Z, CHIPS_Y = 4, 2, 8, 4
ALL_AXES = ("x", "c", "z", "y")
HEAD_AXES = ("c", "y")
ROW_AXES = ("x", "z")
PARTS = CORES * CHIPS_Y
GROUP = QUERY_HEADS // KEY_VALUE_HEADS
ROW = CHIPS_Y
STEPS = SPAN // ROW
WINDOW = SPAN + ROW
SLICES = CHIPS_X * CHIPS_Z
PAIR_ROWS = BLOCK_TOKENS + HEAD_SIZE
SLICE_ROWS = PAIR_ROWS // SLICES
PICKS = GROUP * NV
SLOTS = 1 + NS + NV
CALLS = 2
HEADS_A_CALL = GROUP // CALLS
TILES = CORES * WINDOW + HEADS_A_CALL * NV
COUNTS = (4, 6, SLOTS)
FAR_X = (0, 1, -1, 2)

NEG = -1e30
LOG2_SCALE = float(HEAD_SIZE**-0.5 * np.log2(np.e))


def attend_kernel(half, turns, tile_of, bias_of, spot, q_ref, *rest):
    near = rest[: 1 + 2 * STEPS]
    far = rest[1 + 2 * STEPS : -3]
    out_ref, tiles, sem = rest[-3:]
    head = pl.program_id(0) + half * HEADS_A_CALL

    @pl.when(pl.program_id(0) == 0)
    def _():
        copies = []
        for run in range(CORES):
            first = run * WINDOW
            copies.append((near[0].at[run], tiles.at[pl.ds(first + SPAN, ROW)]))
            for step in range(STEPS):
                source = near[1 + 2 * step + run]
                at = first + SPAN - ROW * (step + 1)
                copies.append((source, tiles.at[pl.ds(at, ROW)]))
        x, z = spot[0], spot[1]
        for ref, x_back in zip(far, FAR_X):
            for n in range(CHIPS_Z):
                at_x = (x - x_back + CHIPS_X) % CHIPS_X
                at_z = (z - n + CHIPS_Z) % CHIPS_Z
                first = pl.multiple_of((at_x * CHIPS_Z + at_z) * SLICE_ROWS, SLICE_ROWS)
                count = HEADS_A_CALL * NV
                target = tiles.at[pl.ds(CORES * WINDOW, count), pl.ds(first, SLICE_ROWS)]
                copies.append((ref.at[n], target))
        copies = [
            pltpu.make_async_copy(source, target, sem.at[n])
            for n, (source, target) in enumerate(copies)
        ]
        for copy in copies:
            copy.start()
        for copy in copies:
            copy.wait()

    rows = lax.broadcasted_iota(jnp.int32, (BLOCK_TOKENS, BLOCK_TOKENS), 0)
    cols = lax.broadcasted_iota(jnp.int32, (BLOCK_TOKENS, BLOCK_TOKENS), 1)
    causal = rows <= cols

    def attend(block, count):
        base = (head * PARTS + block) * SLOTS
        where = [tile_of[base + slot] for slot in range(count)]
        keys = jnp.concatenate([tiles[w, :BLOCK_TOKENS, :] for w in where], axis=0)
        values = jnp.concatenate([tiles[w, BLOCK_TOKENS:, :] for w in where], axis=1)
        raw = lax.dot_general(
            keys, q_ref[block], (((1,), (1,)), ((), ())), preferred_element_type=jnp.float32
        )
        scores = [raw[s * BLOCK_TOKENS : (s + 1) * BLOCK_TOKENS] for s in range(count)]
        scores[0] = jnp.where(causal, scores[0], NEG)
        for slot in range(1, count):
            scores[slot] = scores[slot] + bias_of[base + slot]
        best = jnp.max(functools.reduce(jnp.maximum, scores), axis=0, keepdims=True)
        weights = [jnp.exp2((s - best) * LOG2_SCALE) for s in scores]
        total = jnp.sum(functools.reduce(jnp.add, weights), axis=0, keepdims=True)
        probs = jnp.concatenate([w.astype(jnp.bfloat16) for w in weights], axis=0)
        mixed = jnp.dot(values, probs, preferred_element_type=jnp.float32)
        mixed = mixed * (1.0 / total)
        out_ref[block] = mixed.T.astype(jnp.bfloat16)

    for count in COUNTS:

        @pl.when(turns[head] == count)
        def _():
            for block in range(PARTS):
                attend(block, count)


def attend_half(half, turns, tile_of, bias_of, spot, q, near, far):
    block = (PARTS, BLOCK_TOKENS, HEAD_SIZE)
    width = HEADS_A_CALL * HEAD_SIZE
    anywhere = pl.BlockSpec(memory_space=pltpu.HBM)
    return pl.pallas_call(
        functools.partial(attend_kernel, half),
        out_shape=jax.ShapeDtypeStruct((PARTS, BLOCK_TOKENS, width), jnp.bfloat16),
        grid_spec=pltpu.PrefetchScalarGridSpec(
            num_scalar_prefetch=4,
            grid=(HEADS_A_CALL,),
            in_specs=[
                pl.BlockSpec(block, lambda head, *_: (0, 0, head + half * HEADS_A_CALL))
            ]
            + [anywhere] * (len(near) + len(far)),
            out_specs=pl.BlockSpec(block, lambda head, *_: (0, 0, head)),
            scratch_shapes=[
                pltpu.VMEM((TILES, PAIR_ROWS, HEAD_SIZE), jnp.bfloat16),
                pltpu.SemaphoreType.DMA((CORES * (1 + STEPS) + SLICES,)),
            ],
        ),
        compiler_params=pltpu.CompilerParams(
            dimension_semantics=("arbitrary",), vmem_limit_bytes=60 << 20
        ),
        cost_estimate=pl.CostEstimate(
            flops=4 * 32 * 6 * 128**3, bytes_accessed=8 << 20, transcendentals=32 * 6 * 128**2
        ),
        name="attend",
    )(turns, tile_of, bias_of, spot, q, *near, *far)


def split_pairs_kernel(key_ref, value_ref, out_ref):
    for head in range(KEY_VALUE_HEADS):
        columns = slice(head * HEAD_SIZE, (head + 1) * HEAD_SIZE)
        out_ref[head, :BLOCK_TOKENS, :] = key_ref[:, columns]
        out_ref[head, BLOCK_TOKENS:, :] = value_ref[:, columns].T


def split_pairs(keys, values):
    return pl.pallas_call(
        split_pairs_kernel,
        out_shape=jax.ShapeDtypeStruct(
            (KEY_VALUE_HEADS, PAIR_ROWS, HEAD_SIZE), jnp.bfloat16
        ),
        cost_estimate=pl.CostEstimate(flops=0, bytes_accessed=1 << 20, transcendentals=0),
        compiler_params=pltpu.CompilerParams(vmem_limit_bytes=8 << 20),
        name="split_pairs",
    )(keys, values)


def split_heads_kernel(rows, parts, sem):
    width = parts.shape[2]
    copies = [
        pltpu.make_async_copy(rows.at[:, pl.ds(n * width, width)], parts.at[n], sem.at[n])
        for n in range(PARTS)
    ]
    for copy in copies:
        copy.start()
    for copy in copies:
        copy.wait()


def split_heads(rows):
    return pl.pallas_call(
        split_heads_kernel,
        out_shape=jax.ShapeDtypeStruct(
            (PARTS, BLOCK_TOKENS, rows.shape[1] // PARTS), rows.dtype
        ),
        in_specs=[pl.BlockSpec(memory_space=pltpu.HBM)],
        out_specs=pl.BlockSpec(memory_space=pltpu.VMEM),
        scratch_shapes=[pltpu.SemaphoreType.DMA((PARTS,))],
        cost_estimate=pl.CostEstimate(flops=0, bytes_accessed=4 << 20, transcendentals=0),
        compiler_params=pltpu.CompilerParams(vmem_limit_bytes=8 << 20),
        name="split_heads",
    )(rows)


def merge_heads_kernel(*refs):
    halves, rows, sem = refs[:CALLS], refs[CALLS], refs[CALLS + 1]
    width = halves[0].shape[2]
    copies = []
    for n in range(PARTS):
        for half, parts in enumerate(halves):
            place = n * CALLS + half
            columns = rows.at[:, pl.ds(place * width, width)]
            copies.append(pltpu.make_async_copy(parts.at[n], columns, sem.at[place]))
    for copy in copies:
        copy.start()
    for copy in copies:
        copy.wait()


def merge_heads(*halves):
    return pl.pallas_call(
        merge_heads_kernel,
        out_shape=jax.ShapeDtypeStruct(
            (BLOCK_TOKENS, QUERY_HEADS * HEAD_SIZE), halves[0].dtype
        ),
        in_specs=[pl.BlockSpec(memory_space=pltpu.VMEM)] * CALLS,
        out_specs=pl.BlockSpec(memory_space=pltpu.HBM),
        scratch_shapes=[pltpu.SemaphoreType.DMA((PARTS * CALLS,))],
        cost_estimate=pl.CostEstimate(flops=0, bytes_accessed=4 << 20, transcendentals=0),
        compiler_params=pltpu.CompilerParams(vmem_limit_bytes=8 << 20),
        name="merge_heads",
    )(*halves)


def cut_kernel(tiles, slices):
    for n in range(SLICES):
        slices[n] = tiles[:, n * SLICE_ROWS : (n + 1) * SLICE_ROWS, :]


def cut_slices(tiles):
    return pl.pallas_call(
        cut_kernel,
        out_shape=jax.ShapeDtypeStruct(
            (SLICES, tiles.shape[0], SLICE_ROWS, HEAD_SIZE), tiles.dtype
        ),
        cost_estimate=pl.CostEstimate(flops=0, bytes_accessed=1 << 20, transcendentals=0),
        compiler_params=pltpu.CompilerParams(vmem_limit_bytes=8 << 20),
        name="cut_slices",
    )(tiles)


def stack_kernel(*refs):
    halves = refs[CHIPS_Z:]
    count = HEADS_A_CALL * NV
    for n, ref in enumerate(refs[:CHIPS_Z]):
        for half in range(CALLS):
            halves[half][n] = ref[half * count : (half + 1) * count]


def stack_halves(parts):
    shape = (CHIPS_Z, HEADS_A_CALL * NV, SLICE_ROWS, HEAD_SIZE)
    return pl.pallas_call(
        stack_kernel,
        out_shape=(jax.ShapeDtypeStruct(shape, parts[0].dtype),) * CALLS,
        cost_estimate=pl.CostEstimate(flops=0, bytes_accessed=2 << 20, transcendentals=0),
        compiler_params=pltpu.CompilerParams(vmem_limit_bytes=8 << 20),
        name="stack_halves",
    )(*parts)


def slot_tables(vert, slash, first_blocks, z):
    slash_count = jnp.sum((slash >= 1).astype(jnp.int32), axis=1)
    vert_count = jnp.sum((vert >= 0).astype(jnp.int32), axis=1)
    turns = 1 + slash_count + vert_count
    turns = sum(
        jnp.where(turns > low, high - low, 0) for low, high in zip((0, *COUNTS), COUNTS)
    )
    part = np.arange(PARTS)
    numbers = first_blocks[part // ROW] + (part % ROW)
    own = jnp.asarray(part // ROW * WINDOW + SPAN + part % ROW, jnp.int32)
    inside = jnp.asarray(SPAN + part % ROW, jnp.int32)[None, :, None]
    inside = inside - jnp.maximum(slash, 0)[:, None, :]
    back = STEPS - inside // ROW
    run = jnp.asarray(part // ROW, jnp.int32)[None, :, None]
    held_in = jnp.where(z < back, CORES - 1 - run, run)
    near_tile = held_in * WINDOW + inside
    near_ok = (slash[:, None, :] >= 1) & (numbers[None, :, None] >= slash[:, None, :])
    far_tile = np.arange(PICKS, dtype=np.int32).reshape(GROUP, 1, NV) % (HEADS_A_CALL * NV)
    far_tile = CORES * WINDOW + far_tile
    far_tile = jnp.broadcast_to(far_tile, (GROUP, PARTS, NV))
    hit = jnp.any(
        near_ok[:, :, :, None]
        & (
            numbers[None, :, None, None] - slash[:, None, :, None]
            == vert[:, None, None, :]
        ),
        axis=2,
    )
    far_ok = (
        (vert[:, None, :] >= 0)
        & (vert[:, None, :] < numbers[None, :, None])
        & jnp.logical_not(hit)
    )
    own_tile = jnp.broadcast_to(own[None, :, None], (GROUP, PARTS, 1))
    tile = jnp.concatenate([own_tile, near_tile, far_tile], axis=2)
    fine = jnp.concatenate([jnp.ones((GROUP, PARTS, 1), bool), near_ok, far_ok], axis=2)
    slot = np.arange(SLOTS)
    listed = jnp.concatenate(
        [jnp.ones((GROUP, 1), bool), slash >= 1, vert >= 0], axis=1
    )
    place = jnp.cumsum(listed.astype(jnp.int32), axis=1) - 1
    chosen = listed[:, :, None] & (place[:, :, None] == slot[None, None, :])
    chosen = chosen[:, None, :, :]
    tile_of = jnp.sum(jnp.where(chosen, tile[:, :, :, None], 0), axis=2)
    good = jnp.any(chosen & fine[:, :, :, None], axis=2)
    bias_of = jnp.where(good, 0.0, NEG).astype(jnp.float32)
    return turns, tile_of.reshape(-1), bias_of.reshape(-1)


def shards(queries, key_state_rows, value_state_rows, vert_blocks, slash_offsets):
    x, z = lax.axis_index("x"), lax.axis_index("z")
    key_head = lax.axis_index("c") * CHIPS_Y + lax.axis_index("y")

    def shifted(value, axis, by):
        count = lax.axis_size(axis)
        return lax.ppermute(value, axis, [(n, (n + by) % count) for n in range(count)])

    pairs = split_pairs(key_state_rows, value_state_rows)
    pairs = lax.all_to_all(pairs, HEAD_AXES, 0, 0, tiled=True)
    own = pairs.reshape(CORES, ROW, PAIR_ROWS, HEAD_SIZE)

    onward = [
        (a * CHIPS_Z + b, (a + (b + 1) // CHIPS_Z) % CHIPS_X * CHIPS_Z + (b + 1) % CHIPS_Z)
        for a in range(CHIPS_X)
        for b in range(CHIPS_Z)
    ]
    def passed_on(first, second):
        return shifted(first, "z", 1), lax.ppermute(second, ROW_AXES, onward)

    sliced = lax.all_to_all(cut_slices(pairs), ROW_AXES, 0, 0, tiled=True)
    vert = lax.dynamic_slice_in_dim(vert_blocks, key_head * GROUP, GROUP, 0)
    slash = lax.dynamic_slice_in_dim(slash_offsets, key_head * GROUP, GROUP, 0)
    runs = jnp.arange(CORES, dtype=jnp.int32)
    first_blocks = ((x * CORES + runs) * CHIPS_Z + z) * ROW
    turns, tile_of, bias_of = slot_tables(vert, slash, first_blocks, z)
    spot = jnp.stack([x, z]).astype(jnp.int32)
    listed = jnp.maximum(vert, 0).reshape(-1)
    place, at_z, at_run = listed % ROW, listed // ROW % CHIPS_Z, listed // (ROW * CHIPS_Z)
    at = (at_run // CORES * CHIPS_Z + at_z) * PARTS + at_run % CORES * ROW + place
    tables = (turns, tile_of, bias_of, spot)
    sliced, tables = lax.optimization_barrier((sliced, tables))
    picked = sliced.reshape(SLICES * PARTS, SLICE_ROWS, HEAD_SIZE)[at]

    queries = split_heads(queries)
    q = lax.all_to_all(queries, HEAD_AXES, 0, 0, tiled=True)

    behind = shifted(picked, "z", 1)
    ahead = [picked]
    chain = [(own[0], own[1])]
    chain += [passed_on(*chain[-1])]
    for step in range(1, CHIPS_Z - 1):
        ahead += [shifted(ahead[-1], "z", -1)]
        if step in (1, 3):
            ahead[-1], chain[-1] = lax.optimization_barrier((ahead[-1], chain[-1]))
            chain += [passed_on(*chain[-1])]
    column = [picked, behind] + ahead[:0:-1]
    column, chain[-1] = lax.optimization_barrier((column, chain[-1]))
    columns = stack_halves(column)
    chain += [passed_on(*chain[-1])]
    _, one, two, three, four = chain
    (lower, upper), far = columns, []
    right, left = shifted(lower, "x", 1), shifted(lower, "x", -1)
    far += [(lower, right, left, shifted(right, "x", 1))]
    left, right = shifted(upper, "x", -1), shifted(upper, "x", 1)
    far[0], four, left = lax.optimization_barrier((far[0], four, left))
    far += [(upper, right, left, shifted(left, "x", -1))]
    near = [own, *one, *two, *three, *four]

    returned = []
    for half in range(CALLS):
        mixed = attend_half(half, *tables, q, near, far[half])
        if half == 0:
            mixed, far[1] = lax.optimization_barrier((mixed, far[1]))
        returned += [lax.all_to_all(mixed, HEAD_AXES, 0, 0, tiled=True)]
    return merge_heads(*returned)


def solution(mesh):
    split = Mesh(mesh.devices.reshape(CHIPS_X, CORES, CHIPS_Z, CHIPS_Y), ALL_AXES)
    rows = P(ALL_AXES, None)
    return jax.shard_map(
        shards,
        mesh=split,
        in_specs=(rows, rows, rows, P(), P()),
        out_specs=rows,
        check_vma=False,
    )
```

```python
import functools

import jax
import jax.numpy as jnp
import numpy as np
from jax import lax
from jax.experimental import pallas as pl
from jax.experimental.pallas import tpu as pltpu
from jax.sharding import Mesh, PartitionSpec as P

QUERY_HEADS = 64
KEY_VALUE_HEADS = 8
HEAD_SIZE = 128
BLOCK_TOKENS = 128
NV = 6
NS = 3
SPAN = 16

CHIPS_X, CORES, CHIPS_Z, CHIPS_Y = 4, 2, 8, 4
ALL_AXES = ("x", "c", "z", "y")
HEAD_AXES = ("c", "y")
ROW_AXES = ("x", "z")
PARTS = CORES * CHIPS_Y
GROUP = QUERY_HEADS // KEY_VALUE_HEADS
ROW = CHIPS_Y
STEPS = SPAN // ROW
WINDOW = SPAN + ROW
SLICES = CHIPS_X * CHIPS_Z
PAIR_ROWS = BLOCK_TOKENS + HEAD_SIZE
SLICE_ROWS = PAIR_ROWS // SLICES
PICKS = GROUP * NV
SLOTS = 1 + NS + NV
CALLS = 2
HEADS_A_CALL = GROUP // CALLS
TILES = CORES * WINDOW + HEADS_A_CALL * NV
COUNTS = (4, 6, SLOTS)
FAR_X = (0, 1, -1, 2)

NEG = -1e30
LOG2_SCALE = float(HEAD_SIZE**-0.5 * np.log2(np.e))


def attend_kernel(half, turns, tile_of, bias_of, spot, q_ref, *rest):
    near = rest[: 1 + 2 * STEPS]
    far = rest[1 + 2 * STEPS : -3]
    out_ref, tiles, sem = rest[-3:]
    head = pl.program_id(0) + half * HEADS_A_CALL

    @pl.when(pl.program_id(0) == 0)
    def _():
        copies = []
        for run in range(CORES):
            first = run * WINDOW
            copies.append((near[0].at[run], tiles.at[pl.ds(first + SPAN, ROW)]))
            for step in range(STEPS):
                source = near[1 + 2 * step + run]
                at = first + SPAN - ROW * (step + 1)
                copies.append((source, tiles.at[pl.ds(at, ROW)]))
        x, z = spot[0], spot[1]
        for ref, x_back in zip(far, FAR_X):
            for n in range(CHIPS_Z):
                at_x = (x - x_back + CHIPS_X) % CHIPS_X
                at_z = (z - n + CHIPS_Z) % CHIPS_Z
                first = pl.multiple_of((at_x * CHIPS_Z + at_z) * SLICE_ROWS, SLICE_ROWS)
                count = HEADS_A_CALL * NV
                target = tiles.at[pl.ds(CORES * WINDOW, count), pl.ds(first, SLICE_ROWS)]
                copies.append((ref.at[n], target))
        copies = [
            pltpu.make_async_copy(source, target, sem.at[n])
            for n, (source, target) in enumerate(copies)
        ]
        for copy in copies:
            copy.start()
        for copy in copies:
            copy.wait()

    rows = lax.broadcasted_iota(jnp.int32, (BLOCK_TOKENS, BLOCK_TOKENS), 0)
    cols = lax.broadcasted_iota(jnp.int32, (BLOCK_TOKENS, BLOCK_TOKENS), 1)
    causal = rows <= cols

    def attend(block, count):
        base = (head * PARTS + block) * SLOTS
        where = [tile_of[base + slot] for slot in range(count)]
        keys = jnp.concatenate([tiles[w, :BLOCK_TOKENS, :] for w in where], axis=0)
        values = jnp.concatenate([tiles[w, BLOCK_TOKENS:, :] for w in where], axis=1)
        raw = lax.dot_general(
            keys, q_ref[block], (((1,), (1,)), ((), ())), preferred_element_type=jnp.float32
        )
        scores = [raw[s * BLOCK_TOKENS : (s + 1) * BLOCK_TOKENS] for s in range(count)]
        scores[0] = jnp.where(causal, scores[0], NEG)
        for slot in range(1, count):
            scores[slot] = scores[slot] + bias_of[base + slot]
        best = jnp.max(functools.reduce(jnp.maximum, scores), axis=0, keepdims=True)
        weights = [jnp.exp2((s - best) * LOG2_SCALE) for s in scores]
        total = jnp.sum(functools.reduce(jnp.add, weights), axis=0, keepdims=True)
        probs = jnp.concatenate([w.astype(jnp.bfloat16) for w in weights], axis=0)
        mixed = jnp.dot(values, probs, preferred_element_type=jnp.float32)
        mixed = mixed * (1.0 / total)
        out_ref[block] = mixed.T.astype(jnp.bfloat16)

    for count in COUNTS:

        @pl.when(turns[head] == count)
        def _():
            for block in range(PARTS):
                attend(block, count)


def attend_half(half, turns, tile_of, bias_of, spot, q, near, far):
    block = (PARTS, BLOCK_TOKENS, HEAD_SIZE)
    width = HEADS_A_CALL * HEAD_SIZE
    anywhere = pl.BlockSpec(memory_space=pltpu.HBM)
    return pl.pallas_call(
        functools.partial(attend_kernel, half),
        out_shape=jax.ShapeDtypeStruct((PARTS, BLOCK_TOKENS, width), jnp.bfloat16),
        grid_spec=pltpu.PrefetchScalarGridSpec(
            num_scalar_prefetch=4,
            grid=(HEADS_A_CALL,),
            in_specs=[
                pl.BlockSpec(block, lambda head, *_: (0, 0, head + half * HEADS_A_CALL))
            ]
            + [anywhere] * (len(near) + len(far)),
            out_specs=pl.BlockSpec(block, lambda head, *_: (0, 0, head)),
            scratch_shapes=[
                pltpu.VMEM((TILES, PAIR_ROWS, HEAD_SIZE), jnp.bfloat16),
                pltpu.SemaphoreType.DMA((CORES * (1 + STEPS) + SLICES,)),
            ],
        ),
        compiler_params=pltpu.CompilerParams(
            dimension_semantics=("arbitrary",), vmem_limit_bytes=60 << 20
        ),
        cost_estimate=pl.CostEstimate(
            flops=4 * 32 * 6 * 128**3, bytes_accessed=8 << 20, transcendentals=32 * 6 * 128**2
        ),
        name="attend",
    )(turns, tile_of, bias_of, spot, q, *near, *far)


def split_pairs_kernel(key_ref, value_ref, out_ref):
    for head in range(KEY_VALUE_HEADS):
        columns = slice(head * HEAD_SIZE, (head + 1) * HEAD_SIZE)
        out_ref[head, :BLOCK_TOKENS, :] = key_ref[:, columns]
        out_ref[head, BLOCK_TOKENS:, :] = value_ref[:, columns].T


def split_pairs(keys, values):
    return pl.pallas_call(
        split_pairs_kernel,
        out_shape=jax.ShapeDtypeStruct(
            (KEY_VALUE_HEADS, PAIR_ROWS, HEAD_SIZE), jnp.bfloat16
        ),
        cost_estimate=pl.CostEstimate(flops=0, bytes_accessed=1 << 20, transcendentals=0),
        compiler_params=pltpu.CompilerParams(vmem_limit_bytes=8 << 20),
        name="split_pairs",
    )(keys, values)


def split_heads_kernel(rows, parts, sem):
    width = parts.shape[2]
    copies = [
        pltpu.make_async_copy(rows.at[:, pl.ds(n * width, width)], parts.at[n], sem.at[n])
        for n in range(PARTS)
    ]
    for copy in copies:
        copy.start()
    for copy in copies:
        copy.wait()


def split_heads(rows):
    return pl.pallas_call(
        split_heads_kernel,
        out_shape=jax.ShapeDtypeStruct(
            (PARTS, BLOCK_TOKENS, rows.shape[1] // PARTS), rows.dtype
        ),
        in_specs=[pl.BlockSpec(memory_space=pltpu.HBM)],
        out_specs=pl.BlockSpec(memory_space=pltpu.VMEM),
        scratch_shapes=[pltpu.SemaphoreType.DMA((PARTS,))],
        cost_estimate=pl.CostEstimate(flops=0, bytes_accessed=4 << 20, transcendentals=0),
        compiler_params=pltpu.CompilerParams(vmem_limit_bytes=8 << 20),
        name="split_heads",
    )(rows)


def merge_heads_kernel(*refs):
    halves, rows, sem = refs[:CALLS], refs[CALLS], refs[CALLS + 1]
    width = halves[0].shape[2]
    copies = []
    for n in range(PARTS):
        for half, parts in enumerate(halves):
            place = n * CALLS + half
            columns = rows.at[:, pl.ds(place * width, width)]
            copies.append(pltpu.make_async_copy(parts.at[n], columns, sem.at[place]))
    for copy in copies:
        copy.start()
    for copy in copies:
        copy.wait()


def merge_heads(*halves):
    return pl.pallas_call(
        merge_heads_kernel,
        out_shape=jax.ShapeDtypeStruct(
            (BLOCK_TOKENS, QUERY_HEADS * HEAD_SIZE), halves[0].dtype
        ),
        in_specs=[pl.BlockSpec(memory_space=pltpu.VMEM)] * CALLS,
        out_specs=pl.BlockSpec(memory_space=pltpu.HBM),
        scratch_shapes=[pltpu.SemaphoreType.DMA((PARTS * CALLS,))],
        cost_estimate=pl.CostEstimate(flops=0, bytes_accessed=4 << 20, transcendentals=0),
        compiler_params=pltpu.CompilerParams(vmem_limit_bytes=8 << 20),
        name="merge_heads",
    )(*halves)


def cut_kernel(tiles, slices):
    for n in range(SLICES):
        slices[n] = tiles[:, n * SLICE_ROWS : (n + 1) * SLICE_ROWS, :]


def cut_slices(tiles):
    return pl.pallas_call(
        cut_kernel,
        out_shape=jax.ShapeDtypeStruct(
            (SLICES, tiles.shape[0], SLICE_ROWS, HEAD_SIZE), tiles.dtype
        ),
        cost_estimate=pl.CostEstimate(flops=0, bytes_accessed=1 << 20, transcendentals=0),
        compiler_params=pltpu.CompilerParams(vmem_limit_bytes=8 << 20),
        name="cut_slices",
    )(tiles)


def stack_kernel(*refs):
    halves = refs[CHIPS_Z:]
    count = HEADS_A_CALL * NV
    for n, ref in enumerate(refs[:CHIPS_Z]):
        for half in range(CALLS):
            halves[half][n] = ref[half * count : (half + 1) * count]


def stack_halves(parts):
    shape = (CHIPS_Z, HEADS_A_CALL * NV, SLICE_ROWS, HEAD_SIZE)
    return pl.pallas_call(
        stack_kernel,
        out_shape=(jax.ShapeDtypeStruct(shape, parts[0].dtype),) * CALLS,
        cost_estimate=pl.CostEstimate(flops=0, bytes_accessed=2 << 20, transcendentals=0),
        compiler_params=pltpu.CompilerParams(vmem_limit_bytes=8 << 20),
        name="stack_halves",
    )(*parts)


def slot_tables(vert, slash, first_blocks, z):
    slash_count = jnp.sum((slash >= 1).astype(jnp.int32), axis=1)
    vert_count = jnp.sum((vert >= 0).astype(jnp.int32), axis=1)
    turns = 1 + slash_count + vert_count
    turns = sum(
        jnp.where(turns > low, high - low, 0) for low, high in zip((0, *COUNTS), COUNTS)
    )
    part = np.arange(PARTS)
    numbers = first_blocks[part // ROW] + (part % ROW)
    own = jnp.asarray(part // ROW * WINDOW + SPAN + part % ROW, jnp.int32)
    inside = jnp.asarray(SPAN + part % ROW, jnp.int32)[None, :, None]
    inside = inside - jnp.maximum(slash, 0)[:, None, :]
    back = STEPS - inside // ROW
    run = jnp.asarray(part // ROW, jnp.int32)[None, :, None]
    held_in = jnp.where(z < back, CORES - 1 - run, run)
    near_tile = held_in * WINDOW + inside
    near_ok = (slash[:, None, :] >= 1) & (numbers[None, :, None] >= slash[:, None, :])
    far_tile = np.arange(PICKS, dtype=np.int32).reshape(GROUP, 1, NV) % (HEADS_A_CALL * NV)
    far_tile = CORES * WINDOW + far_tile
    far_tile = jnp.broadcast_to(far_tile, (GROUP, PARTS, NV))
    hit = jnp.any(
        near_ok[:, :, :, None]
        & (
            numbers[None, :, None, None] - slash[:, None, :, None]
            == vert[:, None, None, :]
        ),
        axis=2,
    )
    far_ok = (
        (vert[:, None, :] >= 0)
        & (vert[:, None, :] < numbers[None, :, None])
        & jnp.logical_not(hit)
    )
    own_tile = jnp.broadcast_to(own[None, :, None], (GROUP, PARTS, 1))
    tile = jnp.concatenate([own_tile, near_tile, far_tile], axis=2)
    fine = jnp.concatenate([jnp.ones((GROUP, PARTS, 1), bool), near_ok, far_ok], axis=2)
    slot = np.arange(SLOTS)
    listed = jnp.concatenate(
        [jnp.ones((GROUP, 1), bool), slash >= 1, vert >= 0], axis=1
    )
    place = jnp.cumsum(listed.astype(jnp.int32), axis=1) - 1
    chosen = listed[:, :, None] & (place[:, :, None] == slot[None, None, :])
    chosen = chosen[:, None, :, :]
    tile_of = jnp.sum(jnp.where(chosen, tile[:, :, :, None], 0), axis=2)
    good = jnp.any(chosen & fine[:, :, :, None], axis=2)
    bias_of = jnp.where(good, 0.0, NEG).astype(jnp.float32)
    return turns, tile_of.reshape(-1), bias_of.reshape(-1)


def shards(queries, key_state_rows, value_state_rows, vert_blocks, slash_offsets):
    x, z = lax.axis_index("x"), lax.axis_index("z")
    key_head = lax.axis_index("c") * CHIPS_Y + lax.axis_index("y")

    def shifted(value, axis, by):
        count = lax.axis_size(axis)
        return lax.ppermute(value, axis, [(n, (n + by) % count) for n in range(count)])

    pairs = split_pairs(key_state_rows, value_state_rows)
    pairs = lax.all_to_all(pairs, HEAD_AXES, 0, 0, tiled=True)
    own = pairs.reshape(CORES, ROW, PAIR_ROWS, HEAD_SIZE)

    onward = [
        (a * CHIPS_Z + b, (a + (b + 1) // CHIPS_Z) % CHIPS_X * CHIPS_Z + (b + 1) % CHIPS_Z)
        for a in range(CHIPS_X)
        for b in range(CHIPS_Z)
    ]
    def passed_on(first, second):
        return shifted(first, "z", 1), lax.ppermute(second, ROW_AXES, onward)

    sliced = lax.all_to_all(cut_slices(pairs), ROW_AXES, 0, 0, tiled=True)
    vert = lax.dynamic_slice_in_dim(vert_blocks, key_head * GROUP, GROUP, 0)
    slash = lax.dynamic_slice_in_dim(slash_offsets, key_head * GROUP, GROUP, 0)
    runs = jnp.arange(CORES, dtype=jnp.int32)
    first_blocks = ((x * CORES + runs) * CHIPS_Z + z) * ROW
    turns, tile_of, bias_of = slot_tables(vert, slash, first_blocks, z)
    spot = jnp.stack([x, z]).astype(jnp.int32)
    listed = jnp.maximum(vert, 0).reshape(-1)
    place, at_z, at_run = listed % ROW, listed // ROW % CHIPS_Z, listed // (ROW * CHIPS_Z)
    at = (at_run // CORES * CHIPS_Z + at_z) * PARTS + at_run % CORES * ROW + place
    tables = (turns, tile_of, bias_of, spot)
    chain = [(own[0], own[1]), passed_on(own[0], own[1])]
    sliced, tables, at, chain = lax.optimization_barrier((sliced, tables, at, chain))
    picked = sliced.reshape(SLICES * PARTS, SLICE_ROWS, HEAD_SIZE)[at]

    queries = split_heads(queries)
    q = lax.all_to_all(queries, HEAD_AXES, 0, 0, tiled=True)

    behind = shifted(picked, "z", 1)
    ahead = [picked]
    chain += [passed_on(*chain[-1])]
    for step in range(1, CHIPS_Z - 1):
        ahead += [shifted(ahead[-1], "z", -1)]
        if step == 3:
            ahead[-1], chain[-1] = lax.optimization_barrier((ahead[-1], chain[-1]))
            chain += [passed_on(*chain[-1])]
    column = [picked, behind] + ahead[:0:-1]
    column, chain[-1] = lax.optimization_barrier((column, chain[-1]))
    columns = stack_halves(column)
    chain += [passed_on(*chain[-1])]
    _, one, two, three, four = chain
    far = [(c, *(shifted(c, "x", by) for by in (1, -1, 2))) for c in columns]
    far[0], four = lax.optimization_barrier((far[0], four))
    near = [own, *one, *two, *three, *four]

    returned = []
    for half in range(CALLS):
        mixed = attend_half(half, *tables, q, near, far[half])
        if half == 0:
            mixed, far[1] = lax.optimization_barrier((mixed, far[1]))
        returned += [lax.all_to_all(mixed, HEAD_AXES, 0, 0, tiled=True)]
    return merge_heads(*returned)


def solution(mesh):
    split = Mesh(mesh.devices.reshape(CHIPS_X, CORES, CHIPS_Z, CHIPS_Y), ALL_AXES)
    rows = P(ALL_AXES, None)
    return jax.shard_map(
        shards,
        mesh=split,
        in_specs=(rows, rows, rows, P(), P()),
        out_specs=rows,
        check_vma=False,
    )
```

```python
import functools

import jax
import jax.numpy as jnp
import numpy as np
from jax import lax
from jax.experimental import pallas as pl
from jax.experimental.pallas import tpu as pltpu
from jax.sharding import Mesh, PartitionSpec as P

QUERY_HEADS = 64
KEY_VALUE_HEADS = 8
HEAD_SIZE = 128
BLOCK_TOKENS = 128
NV = 6
NS = 3
SPAN = 16

CHIPS_X, CORES, CHIPS_Z, CHIPS_Y = 4, 2, 8, 4
ALL_AXES = ("x", "c", "z", "y")
HEAD_AXES = ("c", "y")
ROW_AXES = ("x", "z")
PARTS = CORES * CHIPS_Y
GROUP = QUERY_HEADS // KEY_VALUE_HEADS
ROW = CHIPS_Y
STEPS = SPAN // ROW
WINDOW = SPAN + ROW
SLICES = CHIPS_X * CHIPS_Z
PAIR_ROWS = BLOCK_TOKENS + HEAD_SIZE
SLICE_ROWS = PAIR_ROWS // SLICES
PICKS = GROUP * NV
SLOTS = 1 + NS + NV
CALLS = 2
HEADS_A_CALL = GROUP // CALLS
TILES = CORES * WINDOW + HEADS_A_CALL * NV
COUNTS = (4, 6, SLOTS)
FAR_X = (0, 1, -1, 2)

NEG = -1e30
LOG2_SCALE = float(HEAD_SIZE**-0.5 * np.log2(np.e))


def attend_kernel(half, turns, tile_of, bias_of, spot, q_ref, *rest):
    near = rest[: 1 + 2 * STEPS]
    far = rest[1 + 2 * STEPS : -3]
    out_ref, tiles, sem = rest[-3:]
    head = pl.program_id(0) + half * HEADS_A_CALL

    @pl.when(pl.program_id(0) == 0)
    def _():
        copies = []
        for run in range(CORES):
            first = run * WINDOW
            copies.append((near[0].at[run], tiles.at[pl.ds(first + SPAN, ROW)]))
            for step in range(STEPS):
                source = near[1 + 2 * step + run]
                at = first + SPAN - ROW * (step + 1)
                copies.append((source, tiles.at[pl.ds(at, ROW)]))
        x, z = spot[0], spot[1]
        for ref, x_back in zip(far, FAR_X):
            for n in range(CHIPS_Z):
                at_x = (x - x_back + CHIPS_X) % CHIPS_X
                at_z = (z - n + CHIPS_Z) % CHIPS_Z
                first = pl.multiple_of((at_x * CHIPS_Z + at_z) * SLICE_ROWS, SLICE_ROWS)
                count = HEADS_A_CALL * NV
                target = tiles.at[pl.ds(CORES * WINDOW, count), pl.ds(first, SLICE_ROWS)]
                copies.append((ref.at[n], target))
        copies = [
            pltpu.make_async_copy(source, target, sem.at[n])
            for n, (source, target) in enumerate(copies)
        ]
        for copy in copies:
            copy.start()
        for copy in copies:
            copy.wait()

    rows = lax.broadcasted_iota(jnp.int32, (BLOCK_TOKENS, BLOCK_TOKENS), 0)
    cols = lax.broadcasted_iota(jnp.int32, (BLOCK_TOKENS, BLOCK_TOKENS), 1)
    causal = rows <= cols

    def attend(block, count):
        base = (head * PARTS + block) * SLOTS
        where = [tile_of[base + slot] for slot in range(count)]
        keys = jnp.concatenate([tiles[w, :BLOCK_TOKENS, :] for w in where], axis=0)
        values = jnp.concatenate([tiles[w, BLOCK_TOKENS:, :] for w in where], axis=1)
        raw = lax.dot_general(
            keys, q_ref[block], (((1,), (1,)), ((), ())), preferred_element_type=jnp.float32
        )
        scores = [raw[s * BLOCK_TOKENS : (s + 1) * BLOCK_TOKENS] for s in range(count)]
        scores[0] = jnp.where(causal, scores[0], NEG)
        for slot in range(1, count):
            scores[slot] = scores[slot] + bias_of[base + slot]
        best = jnp.max(functools.reduce(jnp.maximum, scores), axis=0, keepdims=True)
        weights = [jnp.exp2((s - best) * LOG2_SCALE) for s in scores]
        total = jnp.sum(functools.reduce(jnp.add, weights), axis=0, keepdims=True)
        probs = jnp.concatenate([w.astype(jnp.bfloat16) for w in weights], axis=0)
        mixed = jnp.dot(values, probs, preferred_element_type=jnp.float32)
        mixed = mixed * (1.0 / total)
        out_ref[block] = mixed.T.astype(jnp.bfloat16)

    for count in COUNTS:

        @pl.when(turns[head] == count)
        def _():
            for block in range(PARTS):
                attend(block, count)


def attend_half(half, turns, tile_of, bias_of, spot, q, near, far):
    block = (PARTS, BLOCK_TOKENS, HEAD_SIZE)
    width = HEADS_A_CALL * HEAD_SIZE
    anywhere = pl.BlockSpec(memory_space=pltpu.HBM)
    return pl.pallas_call(
        functools.partial(attend_kernel, half),
        out_shape=jax.ShapeDtypeStruct((PARTS, BLOCK_TOKENS, width), jnp.bfloat16),
        grid_spec=pltpu.PrefetchScalarGridSpec(
            num_scalar_prefetch=4,
            grid=(HEADS_A_CALL,),
            in_specs=[
                pl.BlockSpec(block, lambda head, *_: (0, 0, head + half * HEADS_A_CALL))
            ]
            + [anywhere] * (len(near) + len(far)),
            out_specs=pl.BlockSpec(block, lambda head, *_: (0, 0, head)),
            scratch_shapes=[
                pltpu.VMEM((TILES, PAIR_ROWS, HEAD_SIZE), jnp.bfloat16),
                pltpu.SemaphoreType.DMA((CORES * (1 + STEPS) + SLICES,)),
            ],
        ),
        compiler_params=pltpu.CompilerParams(
            dimension_semantics=("arbitrary",), vmem_limit_bytes=60 << 20
        ),
        cost_estimate=pl.CostEstimate(
            flops=4 * 32 * 6 * 128**3, bytes_accessed=8 << 20, transcendentals=32 * 6 * 128**2
        ),
        name="attend",
    )(turns, tile_of, bias_of, spot, q, *near, *far)


def split_pairs_kernel(key_ref, value_ref, out_ref):
    for head in range(KEY_VALUE_HEADS):
        columns = slice(head * HEAD_SIZE, (head + 1) * HEAD_SIZE)
        out_ref[head, :BLOCK_TOKENS, :] = key_ref[:, columns]
        out_ref[head, BLOCK_TOKENS:, :] = value_ref[:, columns].T


def split_pairs(keys, values):
    return pl.pallas_call(
        split_pairs_kernel,
        out_shape=jax.ShapeDtypeStruct(
            (KEY_VALUE_HEADS, PAIR_ROWS, HEAD_SIZE), jnp.bfloat16
        ),
        cost_estimate=pl.CostEstimate(flops=0, bytes_accessed=1 << 20, transcendentals=0),
        compiler_params=pltpu.CompilerParams(vmem_limit_bytes=60 << 20),
        name="split_pairs",
    )(keys, values)


def split_heads_kernel(rows, parts, sem):
    width = parts.shape[2]
    copies = [
        pltpu.make_async_copy(rows.at[:, pl.ds(n * width, width)], parts.at[n], sem.at[n])
        for n in range(PARTS)
    ]
    for copy in copies:
        copy.start()
    for copy in copies:
        copy.wait()


def split_heads(rows):
    return pl.pallas_call(
        split_heads_kernel,
        out_shape=jax.ShapeDtypeStruct(
            (PARTS, BLOCK_TOKENS, rows.shape[1] // PARTS), rows.dtype
        ),
        in_specs=[pl.BlockSpec(memory_space=pltpu.HBM)],
        out_specs=pl.BlockSpec(memory_space=pltpu.VMEM),
        scratch_shapes=[pltpu.SemaphoreType.DMA((PARTS,))],
        cost_estimate=pl.CostEstimate(flops=0, bytes_accessed=4 << 20, transcendentals=0),
        compiler_params=pltpu.CompilerParams(vmem_limit_bytes=8 << 20),
        name="split_heads",
    )(rows)


def merge_heads_kernel(*refs):
    halves, rows, sem = refs[:CALLS], refs[CALLS], refs[CALLS + 1]
    width = halves[0].shape[2]
    copies = []
    for n in range(PARTS):
        for half, parts in enumerate(halves):
            place = n * CALLS + half
            columns = rows.at[:, pl.ds(place * width, width)]
            copies.append(pltpu.make_async_copy(parts.at[n], columns, sem.at[place]))
    for copy in copies:
        copy.start()
    for copy in copies:
        copy.wait()


def merge_heads(*halves):
    return pl.pallas_call(
        merge_heads_kernel,
        out_shape=jax.ShapeDtypeStruct(
            (BLOCK_TOKENS, QUERY_HEADS * HEAD_SIZE), halves[0].dtype
        ),
        in_specs=[pl.BlockSpec(memory_space=pltpu.VMEM)] * CALLS,
        out_specs=pl.BlockSpec(memory_space=pltpu.HBM),
        scratch_shapes=[pltpu.SemaphoreType.DMA((PARTS * CALLS,))],
        cost_estimate=pl.CostEstimate(flops=0, bytes_accessed=4 << 20, transcendentals=0),
        compiler_params=pltpu.CompilerParams(vmem_limit_bytes=8 << 20),
        name="merge_heads",
    )(*halves)


def cut_kernel(tiles, slices):
    for n in range(SLICES):
        slices[n] = tiles[:, n * SLICE_ROWS : (n + 1) * SLICE_ROWS, :]


def cut_slices(tiles):
    return pl.pallas_call(
        cut_kernel,
        out_shape=jax.ShapeDtypeStruct(
            (SLICES, tiles.shape[0], SLICE_ROWS, HEAD_SIZE), tiles.dtype
        ),
        cost_estimate=pl.CostEstimate(flops=0, bytes_accessed=1 << 20, transcendentals=0),
        compiler_params=pltpu.CompilerParams(vmem_limit_bytes=8 << 20),
        name="cut_slices",
    )(tiles)


def stack_kernel(*refs):
    halves = refs[CHIPS_Z:]
    count = HEADS_A_CALL * NV
    for n, ref in enumerate(refs[:CHIPS_Z]):
        for half in range(CALLS):
            halves[half][n] = ref[half * count : (half + 1) * count]


def stack_halves(parts):
    shape = (CHIPS_Z, HEADS_A_CALL * NV, SLICE_ROWS, HEAD_SIZE)
    return pl.pallas_call(
        stack_kernel,
        out_shape=(jax.ShapeDtypeStruct(shape, parts[0].dtype),) * CALLS,
        cost_estimate=pl.CostEstimate(flops=0, bytes_accessed=2 << 20, transcendentals=0),
        compiler_params=pltpu.CompilerParams(vmem_limit_bytes=8 << 20),
        name="stack_halves",
    )(*parts)


def slot_tables(vert, slash, first_blocks, z):
    slash_count = jnp.sum((slash >= 1).astype(jnp.int32), axis=1)
    vert_count = jnp.sum((vert >= 0).astype(jnp.int32), axis=1)
    turns = 1 + slash_count + vert_count
    turns = sum(
        jnp.where(turns > low, high - low, 0) for low, high in zip((0, *COUNTS), COUNTS)
    )
    part = np.arange(PARTS)
    numbers = first_blocks[part // ROW] + (part % ROW)
    own = jnp.asarray(part // ROW * WINDOW + SPAN + part % ROW, jnp.int32)
    inside = jnp.asarray(SPAN + part % ROW, jnp.int32)[None, :, None]
    inside = inside - jnp.maximum(slash, 0)[:, None, :]
    back = STEPS - inside // ROW
    run = jnp.asarray(part // ROW, jnp.int32)[None, :, None]
    held_in = jnp.where(z < back, CORES - 1 - run, run)
    near_tile = held_in * WINDOW + inside
    near_ok = (slash[:, None, :] >= 1) & (numbers[None, :, None] >= slash[:, None, :])
    far_tile = np.arange(PICKS, dtype=np.int32).reshape(GROUP, 1, NV) % (HEADS_A_CALL * NV)
    far_tile = CORES * WINDOW + far_tile
    far_tile = jnp.broadcast_to(far_tile, (GROUP, PARTS, NV))
    hit = jnp.any(
        near_ok[:, :, :, None]
        & (
            numbers[None, :, None, None] - slash[:, None, :, None]
            == vert[:, None, None, :]
        ),
        axis=2,
    )
    far_ok = (
        (vert[:, None, :] >= 0)
        & (vert[:, None, :] < numbers[None, :, None])
        & jnp.logical_not(hit)
    )
    own_tile = jnp.broadcast_to(own[None, :, None], (GROUP, PARTS, 1))
    tile = jnp.concatenate([own_tile, near_tile, far_tile], axis=2)
    fine = jnp.concatenate([jnp.ones((GROUP, PARTS, 1), bool), near_ok, far_ok], axis=2)
    slot = np.arange(SLOTS)
    listed = jnp.concatenate(
        [jnp.ones((GROUP, 1), bool), slash >= 1, vert >= 0], axis=1
    )
    place = jnp.cumsum(listed.astype(jnp.int32), axis=1) - 1
    chosen = listed[:, :, None] & (place[:, :, None] == slot[None, None, :])
    chosen = chosen[:, None, :, :]
    tile_of = jnp.sum(jnp.where(chosen, tile[:, :, :, None], 0), axis=2)
    good = jnp.any(chosen & fine[:, :, :, None], axis=2)
    bias_of = jnp.where(good, 0.0, NEG).astype(jnp.float32)
    return turns, tile_of.reshape(-1), bias_of.reshape(-1)


def shards(queries, key_state_rows, value_state_rows, vert_blocks, slash_offsets):
    x, z = lax.axis_index("x"), lax.axis_index("z")
    key_head = lax.axis_index("c") * CHIPS_Y + lax.axis_index("y")

    def shifted(value, axis, by):
        count = lax.axis_size(axis)
        return lax.ppermute(value, axis, [(n, (n + by) % count) for n in range(count)])

    pairs = split_pairs(key_state_rows, value_state_rows)
    pairs = lax.all_to_all(pairs, HEAD_AXES, 0, 0, tiled=True)
    own = pairs.reshape(CORES, ROW, PAIR_ROWS, HEAD_SIZE)

    onward = [
        (a * CHIPS_Z + b, (a + (b + 1) // CHIPS_Z) % CHIPS_X * CHIPS_Z + (b + 1) % CHIPS_Z)
        for a in range(CHIPS_X)
        for b in range(CHIPS_Z)
    ]
    def passed_on(first, second):
        return shifted(first, "z", 1), lax.ppermute(second, ROW_AXES, onward)

    sliced = lax.all_to_all(cut_slices(pairs), ROW_AXES, 0, 0, tiled=True)
    vert = lax.dynamic_slice_in_dim(vert_blocks, key_head * GROUP, GROUP, 0)
    slash = lax.dynamic_slice_in_dim(slash_offsets, key_head * GROUP, GROUP, 0)
    runs = jnp.arange(CORES, dtype=jnp.int32)
    first_blocks = ((x * CORES + runs) * CHIPS_Z + z) * ROW
    turns, tile_of, bias_of = slot_tables(vert, slash, first_blocks, z)
    spot = jnp.stack([x, z]).astype(jnp.int32)
    listed = jnp.maximum(vert, 0).reshape(-1)
    place, at_z, at_run = listed % ROW, listed // ROW % CHIPS_Z, listed // (ROW * CHIPS_Z)
    at = (at_run // CORES * CHIPS_Z + at_z) * PARTS + at_run % CORES * ROW + place
    tables = (turns, tile_of, bias_of, spot)
    chain = [(own[0], own[1]), passed_on(own[0], own[1])]
    sliced, tables, at, chain = lax.optimization_barrier((sliced, tables, at, chain))
    picked = sliced.reshape(SLICES * PARTS, SLICE_ROWS, HEAD_SIZE)[at]

    queries = split_heads(queries)
    q = lax.all_to_all(queries, HEAD_AXES, 0, 0, tiled=True)

    behind = shifted(picked, "z", 1)
    ahead = [picked]
    chain += [passed_on(*chain[-1])]
    for step in range(1, CHIPS_Z - 1):
        ahead += [shifted(ahead[-1], "z", -1)]
        if step == 3:
            ahead[-1], chain[-1] = lax.optimization_barrier((ahead[-1], chain[-1]))
            chain += [passed_on(*chain[-1])]
    column = [picked, behind] + ahead[:0:-1]
    column, chain[-1] = lax.optimization_barrier((column, chain[-1]))
    columns = stack_halves(column)
    chain += [passed_on(*chain[-1])]
    _, one, two, three, four = chain
    far = [(c, *(shifted(c, "x", by) for by in (1, -1, 2))) for c in columns]
    far[0], four = lax.optimization_barrier((far[0], four))
    near = [own, *one, *two, *three, *four]

    returned = []
    for half in range(CALLS):
        mixed = attend_half(half, *tables, q, near, far[half])
        if half == 0:
            mixed, far[1] = lax.optimization_barrier((mixed, far[1]))
        returned += [lax.all_to_all(mixed, HEAD_AXES, 0, 0, tiled=True)]
    return merge_heads(*returned)


def solution(mesh):
    split = Mesh(mesh.devices.reshape(CHIPS_X, CORES, CHIPS_Z, CHIPS_Y), ALL_AXES)
    rows = P(ALL_AXES, None)
    return jax.shard_map(
        shards,
        mesh=split,
        in_specs=(rows, rows, rows, P(), P()),
        out_specs=rows,
        check_vma=False,
    )
```

```python
import functools

import jax
import jax.numpy as jnp
import numpy as np
from jax import lax
from jax.experimental import pallas as pl
from jax.experimental.pallas import tpu as pltpu
from jax.sharding import Mesh, PartitionSpec as P

QUERY_HEADS = 64
KEY_VALUE_HEADS = 8
HEAD_SIZE = 128
BLOCK_TOKENS = 128
NV = 6
NS = 3
SPAN = 16

CHIPS_X, CORES, CHIPS_Z, CHIPS_Y = 4, 2, 8, 4
ALL_AXES = ("x", "c", "z", "y")
HEAD_AXES = ("c", "y")
ROW_AXES = ("x", "z")
PARTS = CORES * CHIPS_Y
GROUP = QUERY_HEADS // KEY_VALUE_HEADS
ROW = CHIPS_Y
STEPS = SPAN // ROW
WINDOW = SPAN + ROW
SLICES = CHIPS_X * CHIPS_Z
PAIR_ROWS = BLOCK_TOKENS + HEAD_SIZE
SLICE_ROWS = PAIR_ROWS // SLICES
PICKS = GROUP * NV
SLOTS = 1 + NS + NV
CALLS = 2
HEADS_A_CALL = GROUP // CALLS
TILES = CORES * WINDOW + HEADS_A_CALL * NV
COUNTS = (4, 6, SLOTS)
FAR_X = (0, 1, -1, 2)

NEG = -1e30
LOG2_SCALE = float(HEAD_SIZE**-0.5 * np.log2(np.e))


def attend_kernel(half, turns, tile_of, bias_of, spot, q_ref, *rest):
    near = rest[: 1 + 2 * STEPS]
    far = rest[1 + 2 * STEPS : -3]
    out_ref, tiles, sem = rest[-3:]
    head = pl.program_id(0) + half * HEADS_A_CALL

    @pl.when(pl.program_id(0) == 0)
    def _():
        copies = []
        for run in range(CORES):
            first = run * WINDOW
            copies.append((near[0].at[run], tiles.at[pl.ds(first + SPAN, ROW)]))
            for step in range(STEPS):
                source = near[1 + 2 * step + run]
                at = first + SPAN - ROW * (step + 1)
                copies.append((source, tiles.at[pl.ds(at, ROW)]))
        x, z = spot[0], spot[1]
        for ref, x_back in zip(far, FAR_X):
            for n in range(CHIPS_Z):
                at_x = (x - x_back + CHIPS_X) % CHIPS_X
                at_z = (z - n + CHIPS_Z) % CHIPS_Z
                first = pl.multiple_of((at_x * CHIPS_Z + at_z) * SLICE_ROWS, SLICE_ROWS)
                count = HEADS_A_CALL * NV
                target = tiles.at[pl.ds(CORES * WINDOW, count), pl.ds(first, SLICE_ROWS)]
                copies.append((ref.at[n], target))
        copies = [
            pltpu.make_async_copy(source, target, sem.at[n])
            for n, (source, target) in enumerate(copies)
        ]
        for copy in copies:
            copy.start()
        for copy in copies:
            copy.wait()

    rows = lax.broadcasted_iota(jnp.int32, (BLOCK_TOKENS, BLOCK_TOKENS), 0)
    cols = lax.broadcasted_iota(jnp.int32, (BLOCK_TOKENS, BLOCK_TOKENS), 1)
    causal = rows <= cols

    def attend(block, count):
        base = (head * PARTS + block) * SLOTS
        where = [tile_of[base + slot] for slot in range(count)]
        keys = jnp.concatenate([tiles[w, :BLOCK_TOKENS, :] for w in where], axis=0)
        values = jnp.concatenate([tiles[w, BLOCK_TOKENS:, :] for w in where], axis=1)
        raw = lax.dot_general(
            keys, q_ref[block], (((1,), (1,)), ((), ())), preferred_element_type=jnp.float32
        )
        scores = [raw[s * BLOCK_TOKENS : (s + 1) * BLOCK_TOKENS] for s in range(count)]
        scores[0] = jnp.where(causal, scores[0], NEG)
        for slot in range(1, count):
            scores[slot] = scores[slot] + bias_of[base + slot]
        best = jnp.max(functools.reduce(jnp.maximum, scores), axis=0, keepdims=True)
        weights = [jnp.exp2((s - best) * LOG2_SCALE) for s in scores]
        total = jnp.sum(functools.reduce(jnp.add, weights), axis=0, keepdims=True)
        probs = jnp.concatenate([w.astype(jnp.bfloat16) for w in weights], axis=0)
        mixed = jnp.dot(values, probs, preferred_element_type=jnp.float32)
        mixed = mixed * (1.0 / total)
        out_ref[block] = mixed.T.astype(jnp.bfloat16)

    for count in COUNTS:

        @pl.when(turns[head] == count)
        def _():
            for block in range(PARTS):
                attend(block, count)


def attend_half(half, turns, tile_of, bias_of, spot, q, near, far):
    block = (PARTS, BLOCK_TOKENS, HEAD_SIZE)
    width = HEADS_A_CALL * HEAD_SIZE
    anywhere = pl.BlockSpec(memory_space=pltpu.HBM)
    return pl.pallas_call(
        functools.partial(attend_kernel, half),
        out_shape=jax.ShapeDtypeStruct((PARTS, BLOCK_TOKENS, width), jnp.bfloat16),
        grid_spec=pltpu.PrefetchScalarGridSpec(
            num_scalar_prefetch=4,
            grid=(HEADS_A_CALL,),
            in_specs=[
                pl.BlockSpec(block, lambda head, *_: (0, 0, head + half * HEADS_A_CALL))
            ]
            + [anywhere] * (len(near) + len(far)),
            out_specs=pl.BlockSpec(block, lambda head, *_: (0, 0, head)),
            scratch_shapes=[
                pltpu.VMEM((TILES, PAIR_ROWS, HEAD_SIZE), jnp.bfloat16),
                pltpu.SemaphoreType.DMA((CORES * (1 + STEPS) + SLICES,)),
            ],
        ),
        compiler_params=pltpu.CompilerParams(
            dimension_semantics=("arbitrary",), vmem_limit_bytes=60 << 20
        ),
        cost_estimate=pl.CostEstimate(
            flops=4 * 32 * 6 * 128**3, bytes_accessed=8 << 20, transcendentals=32 * 6 * 128**2
        ),
        name="attend",
    )(turns, tile_of, bias_of, spot, q, *near, *far)


def split_pairs_kernel(key_ref, value_ref, out_ref):
    for head in range(KEY_VALUE_HEADS):
        columns = slice(head * HEAD_SIZE, (head + 1) * HEAD_SIZE)
        out_ref[head, :BLOCK_TOKENS, :] = key_ref[:, columns]
        out_ref[head, BLOCK_TOKENS:, :] = value_ref[:, columns].T


def split_pairs(keys, values):
    return pl.pallas_call(
        split_pairs_kernel,
        out_shape=jax.ShapeDtypeStruct(
            (KEY_VALUE_HEADS, PAIR_ROWS, HEAD_SIZE), jnp.bfloat16
        ),
        cost_estimate=pl.CostEstimate(flops=0, bytes_accessed=1 << 20, transcendentals=0),
        compiler_params=pltpu.CompilerParams(vmem_limit_bytes=60 << 20),
        name="split_pairs",
    )(keys, values)


def split_heads_kernel(rows, parts, sem):
    width = parts.shape[2]
    copies = [
        pltpu.make_async_copy(rows.at[:, pl.ds(n * width, width)], parts.at[n], sem.at[n])
        for n in range(PARTS)
    ]
    for copy in copies:
        copy.start()
    for copy in copies:
        copy.wait()


def split_heads(rows):
    return pl.pallas_call(
        split_heads_kernel,
        out_shape=jax.ShapeDtypeStruct(
            (PARTS, BLOCK_TOKENS, rows.shape[1] // PARTS), rows.dtype
        ),
        in_specs=[pl.BlockSpec(memory_space=pltpu.HBM)],
        out_specs=pl.BlockSpec(memory_space=pltpu.VMEM),
        scratch_shapes=[pltpu.SemaphoreType.DMA((PARTS,))],
        cost_estimate=pl.CostEstimate(flops=0, bytes_accessed=4 << 20, transcendentals=0),
        compiler_params=pltpu.CompilerParams(vmem_limit_bytes=8 << 20),
        name="split_heads",
    )(rows)


def merge_heads_kernel(*refs):
    halves, rows, sem = refs[:CALLS], refs[CALLS], refs[CALLS + 1]
    width = halves[0].shape[2]
    copies = []
    for n in range(PARTS):
        for half, parts in enumerate(halves):
            place = n * CALLS + half
            columns = rows.at[:, pl.ds(place * width, width)]
            copies.append(pltpu.make_async_copy(parts.at[n], columns, sem.at[place]))
    for copy in copies:
        copy.start()
    for copy in copies:
        copy.wait()


def merge_heads(*halves):
    return pl.pallas_call(
        merge_heads_kernel,
        out_shape=jax.ShapeDtypeStruct(
            (BLOCK_TOKENS, QUERY_HEADS * HEAD_SIZE), halves[0].dtype
        ),
        in_specs=[pl.BlockSpec(memory_space=pltpu.VMEM)] * CALLS,
        out_specs=pl.BlockSpec(memory_space=pltpu.HBM),
        scratch_shapes=[pltpu.SemaphoreType.DMA((PARTS * CALLS,))],
        cost_estimate=pl.CostEstimate(flops=0, bytes_accessed=4 << 20, transcendentals=0),
        compiler_params=pltpu.CompilerParams(vmem_limit_bytes=8 << 20),
        name="merge_heads",
    )(*halves)


def cut_kernel(tiles, slices):
    for n in range(SLICES):
        slices[n] = tiles[:, n * SLICE_ROWS : (n + 1) * SLICE_ROWS, :]


def cut_slices(tiles):
    return pl.pallas_call(
        cut_kernel,
        out_shape=jax.ShapeDtypeStruct(
            (SLICES, tiles.shape[0], SLICE_ROWS, HEAD_SIZE), tiles.dtype
        ),
        cost_estimate=pl.CostEstimate(flops=0, bytes_accessed=1 << 20, transcendentals=0),
        compiler_params=pltpu.CompilerParams(vmem_limit_bytes=8 << 20),
        name="cut_slices",
    )(tiles)


def stack_kernel(*refs):
    halves = refs[CHIPS_Z:]
    count = HEADS_A_CALL * NV
    for n, ref in enumerate(refs[:CHIPS_Z]):
        for half in range(CALLS):
            halves[half][n] = ref[half * count : (half + 1) * count]


def stack_halves(parts):
    shape = (CHIPS_Z, HEADS_A_CALL * NV, SLICE_ROWS, HEAD_SIZE)
    return pl.pallas_call(
        stack_kernel,
        out_shape=(jax.ShapeDtypeStruct(shape, parts[0].dtype),) * CALLS,
        cost_estimate=pl.CostEstimate(flops=0, bytes_accessed=2 << 20, transcendentals=0),
        compiler_params=pltpu.CompilerParams(vmem_limit_bytes=8 << 20),
        name="stack_halves",
    )(*parts)


def slot_tables(vert, slash, first_blocks, z):
    slash_count = jnp.sum((slash >= 1).astype(jnp.int32), axis=1)
    vert_count = jnp.sum((vert >= 0).astype(jnp.int32), axis=1)
    turns = 1 + slash_count + vert_count
    turns = sum(
        jnp.where(turns > low, high - low, 0) for low, high in zip((0, *COUNTS), COUNTS)
    )
    part = np.arange(PARTS)
    numbers = first_blocks[part // ROW] + (part % ROW)
    own = jnp.asarray(part // ROW * WINDOW + SPAN + part % ROW, jnp.int32)
    inside = jnp.asarray(SPAN + part % ROW, jnp.int32)[None, :, None]
    inside = inside - jnp.maximum(slash, 0)[:, None, :]
    back = STEPS - inside // ROW
    run = jnp.asarray(part // ROW, jnp.int32)[None, :, None]
    held_in = jnp.where(z < back, CORES - 1 - run, run)
    near_tile = held_in * WINDOW + inside
    near_ok = (slash[:, None, :] >= 1) & (numbers[None, :, None] >= slash[:, None, :])
    far_tile = np.arange(PICKS, dtype=np.int32).reshape(GROUP, 1, NV) % (HEADS_A_CALL * NV)
    far_tile = CORES * WINDOW + far_tile
    far_tile = jnp.broadcast_to(far_tile, (GROUP, PARTS, NV))
    hit = jnp.any(
        near_ok[:, :, :, None]
        & (
            numbers[None, :, None, None] - slash[:, None, :, None]
            == vert[:, None, None, :]
        ),
        axis=2,
    )
    far_ok = (
        (vert[:, None, :] >= 0)
        & (vert[:, None, :] < numbers[None, :, None])
        & jnp.logical_not(hit)
    )
    own_tile = jnp.broadcast_to(own[None, :, None], (GROUP, PARTS, 1))
    tile = jnp.concatenate([own_tile, near_tile, far_tile], axis=2)
    fine = jnp.concatenate([jnp.ones((GROUP, PARTS, 1), bool), near_ok, far_ok], axis=2)
    slot = np.arange(SLOTS)
    listed = jnp.concatenate(
        [jnp.ones((GROUP, 1), bool), slash >= 1, vert >= 0], axis=1
    )
    place = jnp.cumsum(listed.astype(jnp.int32), axis=1) - 1
    chosen = listed[:, :, None] & (place[:, :, None] == slot[None, None, :])
    chosen = chosen[:, None, :, :]
    tile_of = jnp.sum(jnp.where(chosen, tile[:, :, :, None], 0), axis=2)
    good = jnp.any(chosen & fine[:, :, :, None], axis=2)
    bias_of = jnp.where(good, 0.0, NEG).astype(jnp.float32)
    return turns, tile_of.reshape(-1), bias_of.reshape(-1)


def shards(queries, key_state_rows, value_state_rows, vert_blocks, slash_offsets):
    x, z = lax.axis_index("x"), lax.axis_index("z")
    key_head = lax.axis_index("c") * CHIPS_Y + lax.axis_index("y")

    def shifted(value, axis, by):
        count = lax.axis_size(axis)
        return lax.ppermute(value, axis, [(n, (n + by) % count) for n in range(count)])

    pairs = split_pairs(key_state_rows, value_state_rows)
    pairs = lax.all_to_all(pairs, HEAD_AXES, 0, 0, tiled=True)
    pairs, queries = lax.optimization_barrier((pairs, split_heads(queries)))
    own = pairs.reshape(CORES, ROW, PAIR_ROWS, HEAD_SIZE)

    onward = [
        (a * CHIPS_Z + b, (a + (b + 1) // CHIPS_Z) % CHIPS_X * CHIPS_Z + (b + 1) % CHIPS_Z)
        for a in range(CHIPS_X)
        for b in range(CHIPS_Z)
    ]
    def passed_on(first, second):
        return shifted(first, "z", 1), lax.ppermute(second, ROW_AXES, onward)

    sliced = lax.all_to_all(cut_slices(pairs), ROW_AXES, 0, 0, tiled=True)
    vert = lax.dynamic_slice_in_dim(vert_blocks, key_head * GROUP, GROUP, 0)
    slash = lax.dynamic_slice_in_dim(slash_offsets, key_head * GROUP, GROUP, 0)
    runs = jnp.arange(CORES, dtype=jnp.int32)
    first_blocks = ((x * CORES + runs) * CHIPS_Z + z) * ROW
    turns, tile_of, bias_of = slot_tables(vert, slash, first_blocks, z)
    spot = jnp.stack([x, z]).astype(jnp.int32)
    listed = jnp.maximum(vert, 0).reshape(-1)
    place, at_z, at_run = listed % ROW, listed // ROW % CHIPS_Z, listed // (ROW * CHIPS_Z)
    at = (at_run // CORES * CHIPS_Z + at_z) * PARTS + at_run % CORES * ROW + place
    tables = (turns, tile_of, bias_of, spot)
    chain = [(own[0], own[1]), passed_on(own[0], own[1])]
    sliced, tables, at, chain = lax.optimization_barrier((sliced, tables, at, chain))
    picked = sliced.reshape(SLICES * PARTS, SLICE_ROWS, HEAD_SIZE)[at]

    q = lax.all_to_all(queries, HEAD_AXES, 0, 0, tiled=True)

    behind = shifted(picked, "z", 1)
    ahead = [picked]
    chain += [passed_on(*chain[-1])]
    for step in range(1, CHIPS_Z - 1):
        ahead += [shifted(ahead[-1], "z", -1)]
        if step == 3:
            ahead[-1], chain[-1] = lax.optimization_barrier((ahead[-1], chain[-1]))
            chain += [passed_on(*chain[-1])]
    column = [picked, behind] + ahead[:0:-1]
    column, chain[-1] = lax.optimization_barrier((column, chain[-1]))
    columns = stack_halves(column)
    chain += [passed_on(*chain[-1])]
    _, one, two, three, four = chain
    far = [(c, *(shifted(c, "x", by) for by in (1, -1, 2))) for c in columns]
    far[0], four = lax.optimization_barrier((far[0], four))
    near = [own, *one, *two, *three, *four]

    returned = []
    for half in range(CALLS):
        mixed = attend_half(half, *tables, q, near, far[half])
        if half == 0:
            mixed, far[1] = lax.optimization_barrier((mixed, far[1]))
        returned += [lax.all_to_all(mixed, HEAD_AXES, 0, 0, tiled=True)]
    return merge_heads(*returned)


def solution(mesh):
    split = Mesh(mesh.devices.reshape(CHIPS_X, CORES, CHIPS_Z, CHIPS_Y), ALL_AXES)
    rows = P(ALL_AXES, None)
    return jax.shard_map(
        shards,
        mesh=split,
        in_specs=(rows, rows, rows, P(), P()),
        out_specs=rows,
        check_vma=False,
    )
```
